32 devices in a mesh: seq: 16 (over z, y, x), mp: 2 (over core).
Axes of the slice: x: 2, y: 2, z: 4, core: 2. Of those that a mesh axis runs over, the one named last changes fastest.
Arguments:
- layer_input: bfloat16 [2, 4096, 2048], P(None, 'seq'), may hold values from -6 to 6
- cotangent: bfloat16 [2, 4096, 2048], P(None, 'seq'), may hold values from -8 to 8
- teacher: bfloat16 [2, 4096, 2048], P(None, 'seq'), may hold values from -12 to 12
- target_slot: int32 [2, 4096], P(None, 'seq'), may hold values from 0 to 4095, as said below
- seq_start: int32 [2, 2], replicated, may hold values from 0 to 4032, as said below
- seq_len: int32 [2, 2], replicated, may hold values from 1 to 4096, as said below
- w_query: bfloat16 [2048, 1024], P('seq', 'mp'), may hold values from -0.125 to 0.125
- w_key: bfloat16 [2048, 1024], P('seq', 'mp'), may hold values from -0.125 to 0.125
- w_value: bfloat16 [2048, 2048], P('seq', 'mp'), may hold values from -0.125 to 0.125
- w_gate_out: bfloat16 [2048, 2048], P('seq', 'mp'), may hold values from -0.125 to 0.125
- w_out: bfloat16 [2048, 2048], P('seq', 'mp'), may hold values from -0.25 to 0.25
- w_ffn_gate: bfloat16 [2048, 5632], P('seq', 'mp'), may hold values from -0.125 to 0.125
- w_ffn_up: bfloat16 [2048, 5632], P('seq', 'mp'), may hold values from -0.125 to 0.125
- w_ffn_down: bfloat16 [2048, 5632], P('seq', 'mp'), may hold values from -0.15625 to 0.15625
- w_rank_down: bfloat16 [2048, 16], P('seq'), may hold values from -0.125 to 0.125
- w_rank_up: bfloat16 [16, 1024], P(None, 'mp'), may hold values from -1.5 to 1.5
- decay_bias: bfloat16 [1024], P('mp'), may hold values from 1 to 9
- gain_attn: bfloat16 [2048], P('seq'), may hold values from 0.5 to 1.5
- gain_ffn: bfloat16 [2048], P('seq'), may hold values from 0.5 to 1.5
- gain_head: bfloat16 [512], replicated, may hold values from 0.5 to 1.5
Outputs:
- output: bfloat16 [2, 4096, 2048], P(None, 'seq')
- loss: float32 [], replicated
- input_grad: bfloat16 [2, 4096, 2048], P(None, 'seq')
- grad_w_query: float32 [2048, 1024], P('seq', 'mp')
- grad_w_key: float32 [2048, 1024], P('seq', 'mp')
- grad_w_value: float32 [2048, 2048], P('seq', 'mp')
- grad_w_gate_out: float32 [2048, 2048], P('seq', 'mp')
- grad_w_out: float32 [2048, 2048], P('seq', 'mp')
- grad_w_ffn_gate: float32 [2048, 5632], P('seq', 'mp')
- grad_w_ffn_up: float32 [2048, 5632], P('seq', 'mp')
- grad_w_ffn_down: float32 [2048, 5632], P('seq', 'mp')
- grad_w_rank_down: float32 [2048, 16], P('seq')
- grad_w_rank_up: float32 [16, 1024], P(None, 'mp')
- grad_decay_bias: float32 [1024], P('mp')
- grad_gain_attn: float32 [2048], P('seq')
- grad_gain_ffn: float32 [2048], P('seq')
- grad_gain_head: float32 [512], replicated
The draws below stay inside these ranges and needn't reach their ends.
Inputs may be any that keep to these rules, and one draw needn't show every extreme that they name: `target_slot`: for each micro-batch a permutation of the layout slots; the tokens that one index of seq holds go in groups of exactly 32 to half of the indices of seq and to no others, which ones drawn from the seed. `seq_start`: in each micro-batch the sequences lie one after another from layout slot 0, each beginning at a multiple of 64, the first at 0, the last region ending at 4096; one sequence of each micro-batch, drawn from the seed, begins on the first index of seq and has valid tokens on the last. The maximum bounds the range and is not a buffer bound. `seq_len`: A sequence's valid tokens fill its region from the front and leave fewer than 64 slots at its end. The maximum bounds the range and is not a buffer bound.
All inputs are finite; a program needn't handle non-finite values.
Results may differ from the reference program's by a relative error of at most 0.014.
The reference program's roundings to bfloat16 on the way count: a program that leaves them out, or rounds other values in their place, can miss the bound.
Values may be sent and summed in bfloat16 or wider, within the bound.
A program may use at most 448 MiB of HBM per device.

```python
import jax
import jax.numpy as jnp
from jax import lax

D = 2048
HEADS = 4
KEY_DIM = 1024
VALUE_DIM = 2048
FF = 5632
RANK = 16
SPAN = 64
HEAD_K = 256
HEAD_V = 512
TOK_MB = 256
MICRO = 2
SEQS = 2
SLOTS = 4096


def draw_teacher(key, part):
    positions = jnp.arange(SLOTS)
    devices = SLOTS // TOK_MB
    fraction = (positions // TOK_MB).astype(jnp.float32) / max(devices - 1, 1)
    base = jnp.clip(jax.random.normal(key, (MICRO, SLOTS, D), jnp.float32), -4.0, 4.0)
    scaling = 1.0 + 2.0 * fraction
    return (base * scaling[None, :, None]).astype(jnp.bfloat16)


def shuffle_row(row_key):
    return jax.random.permutation(row_key, TOK_MB)


def route_batch(subkey):
    devices = SLOTS // TOK_MB
    groups = devices // 2
    per_pair = TOK_MB // groups
    shift_key, home_key, land_key = jax.random.split(subkey, 3)
    shifts = jax.random.permutation(shift_key, devices)[:groups]
    home_order = jax.vmap(shuffle_row)(jax.random.split(home_key, devices))
    landing = jax.vmap(shuffle_row)(jax.random.split(land_key, devices))
    group_index = home_order // per_pair
    within = home_order % per_pair
    home_ids = jnp.arange(devices)[:, None]
    destination = (home_ids - shifts[group_index]) % devices
    placed = landing[destination, group_index * per_pair + within]
    return (destination * TOK_MB + placed).reshape(-1).astype(jnp.int32)


def draw_target_slot(key, part):
    return jax.vmap(route_batch)(jax.random.split(jax.random.fold_in(key, 11), MICRO))


def plan_batch(subkey):
    blocks = TOK_MB // SPAN
    total_blocks = SLOTS // SPAN
    limit = (blocks - 1) // (SEQS - 1)
    pick_key, size_key, pad_key = jax.random.split(subkey, 3)
    longest = jax.random.randint(pick_key, (), 0, SEQS)
    sizes = jax.random.randint(size_key, (SEQS,), 1, limit + 1)
    order_ids = jnp.arange(SEQS)
    others = jnp.sum(jnp.where(order_ids == longest, 0, sizes))
    sizes = jnp.where(order_ids == longest, total_blocks - others, sizes)
    starts = (jnp.cumsum(sizes) - sizes) * SPAN
    pads = jax.random.randint(pad_key, (SEQS,), 0, SPAN)
    return (starts.astype(jnp.int32), (sizes * SPAN - pads).astype(jnp.int32))


def sequence_plan(key):
    return jax.vmap(plan_batch)(jax.random.split(jax.random.fold_in(key, 7), MICRO))


def draw_seq_start(key, part):
    return sequence_plan(key)[0]


def draw_seq_len(key, part):
    return sequence_plan(key)[1]


def strengthened(entries, own_key, source, target, parts, factor):
    owner, partner = [(jnp.arange(entries.shape[position]) // (entries.shape[position] // parts)).reshape([-1 if axis == position else 1 for axis in range(entries.ndim)]) for position in (source, target)]
    chosen = jax.random.permutation(own_key, parts)[partner]
    strong = (owner == chosen) | (owner == (partner + parts // 2) % parts)
    return jnp.where(strong, factor * entries, entries)


def block_scale(own_key, shape, cuts, low, high):
    def one(axis_at, blocks):
        heights = jax.random.uniform(jax.random.fold_in(jax.random.fold_in(own_key, 6), axis_at), (blocks,), jnp.float32, low / len(cuts), high / len(cuts))
        return jnp.repeat(jnp.exp(heights), shape[axis_at] // blocks).reshape((-1,) + (1,) * (len(shape) - axis_at - 1))

    gain = one(*cuts[0])
    for cut in cuts[1:]:
        gain = gain * one(*cut)
    return gain


def centred(rng, extent, width, reach, cuts=(), held_as=jnp.bfloat16):
    array = width * jax.random.normal(rng, extent, jnp.float32)
    if cuts:
        array = array * block_scale(rng, extent, cuts, -0.22, 0.18)
    return jnp.clip(array, -reach, reach).astype(held_as)


def gaussian_with(stream_key, shape, scale, most, cuts, heavy, kind=jnp.bfloat16):
    values = scale * jax.random.normal(stream_key, shape, jnp.float32)
    if cuts:
        values = values * block_scale(stream_key, shape, cuts, -0.22, 0.18)
    return jnp.clip(strengthened(values, jax.random.fold_in(stream_key, 3), *heavy), -most, most).astype(kind)


def setup_inputs(seed: int = 0) -> dict:
    key_of = jax.random.split(jax.random.key(seed), 21)
    layer_input = centred(key_of[0], (MICRO, SLOTS, D), 1.0, 6.0, ((1, 16),))
    cotangent = gaussian_with(key_of[1], (MICRO, SLOTS, D), 1.0, 8.0, ((1, 16),), (1, 2, 16, 2.0))
    teacher = draw_teacher(jax.random.fold_in(key_of[20], 71), 0)
    target_slot = draw_target_slot(jax.random.fold_in(key_of[20], 71), 0)
    seq_start = draw_seq_start(jax.random.fold_in(key_of[20], 71), 0)
    seq_len = draw_seq_len(jax.random.fold_in(key_of[20], 71), 0)
    w_query = centred(key_of[6], (D, KEY_DIM), D ** -0.5, 0.125, ((0, 16), (1, 2)))
    w_key = centred(key_of[7], (D, KEY_DIM), D ** -0.5, 0.125, ((0, 16), (1, 2)))
    w_value = centred(key_of[8], (D, VALUE_DIM), D ** -0.5, 0.125, ((0, 16), (1, 2)))
    w_gate_out = centred(key_of[9], (D, VALUE_DIM), D ** -0.5, 0.125, ((0, 16), (1, 2)))
    w_out = centred(key_of[10], (D, VALUE_DIM), (VALUE_DIM // 4) ** -0.5, 0.25, ((0, 16), (1, 2)))
    w_ffn_gate = centred(key_of[11], (D, FF), D ** -0.5, 0.125, ((0, 16), (1, 2)))
    w_ffn_up = centred(key_of[12], (D, FF), D ** -0.5, 0.125, ((0, 16), (1, 2)))
    w_ffn_down = centred(key_of[13], (D, FF), (FF // 4) ** -0.5, 0.15625, ((0, 16), (1, 2)))
    w_rank_down = centred(key_of[14], (D, RANK), D ** -0.5, 0.125, ((0, 16),))
    w_rank_up = centred(key_of[15], (RANK, KEY_DIM), RANK ** -0.5, 1.5, ((1, 2),))
    decay_bias = jnp.clip(1.0 + 8.0 * jax.random.uniform(key_of[16], (KEY_DIM,), jnp.float32) ** block_scale(key_of[16], (KEY_DIM,), ((0, 2),), -0.2, 0.2), 1.0, 9.0).astype(jnp.bfloat16)
    gain_attn = jnp.clip(1.0 + 0.1 * jax.random.normal(key_of[17], (D,), jnp.float32), 0.5, 1.5).astype(jnp.bfloat16)
    gain_ffn = jnp.clip(1.0 + 0.1 * jax.random.normal(key_of[18], (D,), jnp.float32), 0.5, 1.5).astype(jnp.bfloat16)
    gain_head = jnp.clip(1.0 + 0.1 * jax.random.normal(key_of[19], (HEAD_V,), jnp.float32), 0.5, 1.5).astype(jnp.bfloat16)
    return {"layer_input": layer_input, "cotangent": cotangent, "teacher": teacher, "target_slot": target_slot, "seq_start": seq_start, "seq_len": seq_len, "w_query": w_query, "w_key": w_key, "w_value": w_value, "w_gate_out": w_gate_out, "w_out": w_out, "w_ffn_gate": w_ffn_gate, "w_ffn_up": w_ffn_up, "w_ffn_down": w_ffn_down, "w_rank_down": w_rank_down, "w_rank_up": w_rank_up, "decay_bias": decay_bias, "gain_attn": gain_attn, "gain_ffn": gain_ffn, "gain_head": gain_head}


eps = 1e-06
highest = lax.Precision.HIGHEST

@jax.custom_vjp
def low(v):
    return lax.optimization_barrier(v.astype(jnp.bfloat16)).astype(jnp.float32)

@jax.custom_vjp
def low_back(v):
    return v

def low_keep(v):
    return (low(v), None)

def low_pass(kept, grad):
    return (grad,)

def back_keep(v):
    return (v, None)

def back_low(kept, grad):
    return (low(grad),)
low.defvjp(low_keep, low_pass)
low_back.defvjp(back_keep, back_low)

def rms_scale(values):
    return lax.rsqrt(lax.optimization_barrier(jnp.mean(values * values, axis=-1, keepdims=True)) + eps)

def head_scale(values):
    return lax.rsqrt(jnp.maximum(lax.optimization_barrier(jnp.mean(values * values, axis=-1, keepdims=True)), 1.0))

def layout_flags(starts, lengths, positions):
    begun = (positions[:, None] >= starts[None, :]).astype(jnp.int32)
    owner = lax.optimization_barrier(jnp.sum(begun, axis=1)) - 1
    picked = (owner[:, None] == jnp.arange(starts.shape[0], dtype=jnp.int32)[None, :]).astype(jnp.int32)
    own_start = lax.optimization_barrier(jnp.sum(picked * starts[None, :], axis=1))
    own_length = lax.optimization_barrier(jnp.sum(picked * lengths[None, :], axis=1))
    valid = (positions - own_start < own_length).astype(jnp.float32)
    boundary = jnp.any(positions[:, None] == starts[None, :], axis=1).astype(jnp.float32)
    return (valid, boundary)

def span_step(carried, pieces):
    queries, key_rows, value_rows, decays, reset = pieces
    before = carried * (1.0 - reset)
    cumul = jnp.cumsum(decays, axis=0)
    lifted = queries * jnp.exp(cumul)
    lowered = key_rows * jnp.exp(-cumul)
    scores = jnp.einsum('thc,shc->hts', lifted, lowered, precision=highest)
    length = decays.shape[0]
    causal = (jnp.arange(length)[:, None] >= jnp.arange(length)[None, :]).astype(jnp.float32)
    mixed = jnp.einsum('hts,shv->thv', scores * causal[None], value_rows, precision=highest)
    mixed = mixed + jnp.einsum('thc,hcv->thv', lifted, before, precision=highest)
    final = cumul[-1]
    faded = key_rows * jnp.exp(final[None] - cumul)
    after = jnp.exp(final)[:, :, None] * before + jnp.einsum('thc,thv->hcv', faded, value_rows, precision=highest)
    return (after, mixed)

def layer_forward(inputs, weights, valid, resets):
    query_weight, key_weight, value_weight, gate_weight, out_weight, ffn_gate_weight, ffn_up_weight, ffn_down_weight, rank_down_weight, rank_up_weight, bias_values, attn_gain, ffn_gain, head_gain = weights
    rows = inputs.shape[0]
    blocks = rows // SPAN
    normed = low(inputs * rms_scale(inputs) * attn_gain)
    query_proj = low_back(jnp.dot(normed, query_weight, precision=highest))
    key_proj = low_back(jnp.dot(normed, key_weight, precision=highest))
    value_proj = low_back(jnp.dot(normed, value_weight, precision=highest))
    gate_pre = low_back(jnp.dot(normed, gate_weight, precision=highest))
    rank_rows = low_back(jnp.dot(normed, rank_down_weight, precision=highest))
    logits = jnp.dot(rank_rows, rank_up_weight, precision=highest) + bias_values
    decays = (jax.nn.log_sigmoid(logits) / 16.0).reshape(blocks, SPAN, HEADS, HEAD_K)
    queries = (query_proj * HEAD_K ** (-0.5)).reshape(blocks, SPAN, HEADS, HEAD_K)
    key_rows = key_proj.reshape(blocks, SPAN, HEADS, HEAD_K)
    value_rows = value_proj.reshape(blocks, SPAN, HEADS, HEAD_V)
    initial = jnp.zeros((HEADS, HEAD_K, HEAD_V), jnp.float32)
    _, mixed = lax.scan(jax.checkpoint(span_step), initial, (queries, key_rows, value_rows, decays, resets))
    mixed = mixed.reshape(rows, HEADS, HEAD_V)
    head_normed = (mixed * head_scale(mixed) * head_gain).reshape(rows, VALUE_DIM)
    gated = low(head_normed * jax.nn.silu(gate_pre))
    attended = low_back(jnp.dot(gated, out_weight.T, precision=highest))
    hidden = inputs + attended
    normed_two = low(hidden * rms_scale(hidden) * ffn_gain)
    gating = low_back(jnp.dot(normed_two, ffn_gate_weight, precision=highest))
    upward = low_back(jnp.dot(normed_two, ffn_up_weight, precision=highest))
    product = low(jax.nn.silu(gating) * upward)
    ffn_out = low_back(jnp.dot(product, ffn_down_weight.T, precision=highest))
    return (hidden + ffn_out) * valid[:, None]

def reference(layer_input, cotangent, teacher, target_slot, seq_start, seq_len, w_query, w_key, w_value, w_gate_out, w_out, w_ffn_gate, w_ffn_up, w_ffn_down, w_rank_down, w_rank_up, decay_bias, gain_attn, gain_ffn, gain_head):
    params = tuple((weight.astype(jnp.float32) for weight in (w_query, w_key, w_value, w_gate_out, w_out, w_ffn_gate, w_ffn_up, w_ffn_down, w_rank_down, w_rank_up, decay_bias, gain_attn, gain_ffn, gain_head)))
    positions = jnp.arange(SLOTS, dtype=jnp.int32)
    count = jnp.sum(seq_len).astype(jnp.float32)
    outputs = []
    input_grads = []
    totals = None
    loss_sum = jnp.zeros((), jnp.float32)
    for micro_index in range(MICRO):
        targets = target_slot[micro_index].astype(jnp.int32)
        inverse = jnp.zeros((SLOTS,), jnp.int32).at[targets].set(positions)
        rows = layer_input[micro_index].astype(jnp.float32)[inverse]
        upstream = cotangent[micro_index].astype(jnp.float32)[inverse]
        valid, boundary = layout_flags(seq_start[micro_index], seq_len[micro_index], positions)
        resets = boundary.reshape(-1, SPAN)[:, 0]

        def forward_rows(inputs, weights):
            return layer_forward(inputs, weights, valid, resets)
        result, pullback = jax.vjp(forward_rows, rows, params)
        d_rows, d_params = pullback(upstream)
        home = result[targets].astype(jnp.bfloat16)
        outputs.append(home)
        input_grads.append(d_rows[targets].astype(jnp.bfloat16))
        difference = home.astype(jnp.float32) - teacher[micro_index].astype(jnp.float32)
        loss_sum = loss_sum + jnp.sum(valid[targets][:, None] * difference * difference)
        totals = d_params if totals is None else jax.tree.map(jnp.add, totals, d_params)
    loss = loss_sum / (count * D)
    return (jnp.stack(outputs), loss, jnp.stack(input_grads), totals[0], totals[1], totals[2], totals[3], totals[4], totals[5], totals[6], totals[7], totals[8], totals[9], totals[10], totals[11], totals[12], totals[13])
```

```python
import functools

import jax
import jax.numpy as jnp
from jax import lax
from jax.experimental import pallas as pl
from jax.experimental.pallas import tpu as pltpu
from jax.sharding import Mesh
from jax.sharding import PartitionSpec as P

SPAN = 64
HEAD_K = 256
HEAD_V = 512
GROUP = 4
LANES = 128

eps = 1e-06
highest = lax.Precision.HIGHEST
contract_last = (((1,), (1,)), ((), ()))
contract_rows = (((0,), (0,)), ((), ()))
bf16 = jnp.bfloat16
f32 = jnp.float32


def rms_scale(values):
    return lax.rsqrt(jnp.mean(values * values, axis=-1, keepdims=True) + eps)


def layout_valid(starts, lengths, positions):
    begun = (positions[:, None] >= starts[None, :]).astype(jnp.int32)
    owner = jnp.sum(begun, axis=1) - 1
    ids = jnp.arange(starts.shape[0], dtype=jnp.int32)
    picked = (owner[:, None] == ids[None, :]).astype(jnp.int32)
    own_start = jnp.sum(picked * starts[None, :], axis=1)
    own_length = jnp.sum(picked * lengths[None, :], axis=1)
    return (positions - own_start < own_length).astype(f32)


def project(left, right):
    return jnp.dot(left, right, preferred_element_type=f32)


def project_back(left, right):
    return lax.dot_general(left, right, contract_last, preferred_element_type=f32)


def outer_sum(left, right):
    return lax.dot_general(left, right, contract_rows, preferred_element_type=f32)


def norm_back(grad_unit, unit, scaling):
    return scaling * (grad_unit - unit * jnp.mean(grad_unit * unit, axis=-1, keepdims=True))


def exact(left, right, dims):
    return lax.dot_general(left, right, dims, precision=highest, preferred_element_type=f32)


plain = (((1,), (0,)), ((), ()))


def triangle(upper):
    row = lax.broadcasted_iota(jnp.int32, (SPAN, SPAN), 0)
    col = lax.broadcasted_iota(jnp.int32, (SPAN, SPAN), 1)
    return jnp.where(col >= row if upper else row >= col, 1.0, 0.0).astype(f32)


def kept(resets, block):
    return jnp.where(resets[block] == 1, 0.0, 1.0)


def states_kernel(order, resets, key_ref, value_ref, decay_ref, cumul_ref, left_ref, state, through):
    block = pl.program_id(0)

    @pl.when(block == 0)
    def _():
        state[...] = jnp.zeros_like(state)
        through[...] = jnp.ones_like(through)

    cumul = exact(triangle(False), decay_ref[...], plain)
    cumul_ref[...] = cumul
    last = cumul[SPAN - 1 : SPAN, :]
    faded = key_ref[...] * jnp.exp(last - cumul)
    fade = jnp.exp(last) * kept(resets, block)
    state[...] = state[...] * fade + exact(value_ref[...], faded, contract_rows)
    through[...] = through[...] * fade

    @pl.when(block == pl.num_programs(0) - 1)
    def _():
        left_ref[:HEAD_V, :] = state[...]
        left_ref[HEAD_V:, :] = through[...]


def mix_kernel(
    order, resets, query_ref, key_ref, value_ref, gate_ref, cumul_ref, gain_ref, enter_ref,
    gated_ref, mixed_ref, saved_ref, state,
):
    block = pl.program_id(0)

    @pl.when(block == 0)
    def _():
        state[...] = enter_ref[...]

    cumul = cumul_ref[...]
    last = cumul[SPAN - 1 : SPAN, :]
    key_rows = key_ref[...]
    value_rows = value_ref[...]
    lifted = query_ref[...] * (HEAD_K ** (-0.5)) * jnp.exp(cumul)
    lowered = key_rows * jnp.exp(-cumul)
    before = state[...] * kept(resets, block)
    saved_ref[0] = before
    scores = exact(lifted, lowered, contract_last) * triangle(False)
    mixed = exact(scores, value_rows, plain) + exact(lifted, before, contract_last)
    mixed_ref[...] = mixed
    faded = key_rows * jnp.exp(last - cumul)
    state[...] = before * jnp.exp(last) + exact(value_rows, faded, contract_rows)
    square = jnp.mean(mixed * mixed, axis=-1, keepdims=True)
    unit = mixed * lax.rsqrt(jnp.maximum(square, 1.0))
    gate = gate_ref[...]
    gated_ref[...] = (unit * gain_ref[...] * (gate * jax.nn.sigmoid(gate))).astype(bf16)


def pull_kernel(
    order, resets, query_ref, gate_ref, cumul_ref, mixed_ref, grad_ref, gain_ref,
    d_mixed_ref, d_gate_ref, head_ref, pulled_ref, through,
):
    block = pl.program_id(0)

    @pl.when(block == 0)
    def _():
        through[...] = jnp.ones_like(through)
        pulled_ref[...] = jnp.zeros_like(pulled_ref)
        head_ref[...] = jnp.zeros_like(head_ref)

    cumul = cumul_ref[...]
    mixed = mixed_ref[...]
    gate = gate_ref[...]
    grad = grad_ref[...]
    gain = gain_ref[...]
    square = jnp.mean(mixed * mixed, axis=-1, keepdims=True)
    scale = lax.rsqrt(jnp.maximum(square, 1.0))
    free = jnp.where(square > 1.0, 1.0, 0.0)
    unit = mixed * scale
    sig = jax.nn.sigmoid(gate)
    d_head = grad * (gate * sig)
    d_gate_ref[...] = (grad * (unit * gain) * sig * (1.0 + gate * (1.0 - sig))).astype(bf16)
    head_ref[...] += jnp.sum((d_head * unit).reshape(SPAN // 8, 8, HEAD_V), axis=0)
    scaled = d_head * gain
    d_mixed = scale * (scaled - free * unit * jnp.mean(scaled * unit, axis=-1, keepdims=True))
    d_mixed_ref[...] = d_mixed
    opened = through[...] * kept(resets, block)
    lifted = query_ref[...] * (HEAD_K ** (-0.5)) * jnp.exp(cumul)
    pulled_ref[...] += exact(d_mixed, lifted * opened[:1, :], contract_rows)
    through[...] = opened * jnp.exp(cumul[SPAN - 1 : SPAN, :])


def back_kernel(
    order, resets, query_ref, key_ref, value_ref, cumul_ref, saved_ref, d_mixed_ref, d_gate_ref, later_ref,
    grads_ref, d_decay_ref, state,
):
    step = pl.program_id(0)
    block = pl.num_programs(0) - 1 - step

    @pl.when(step == 0)
    def _():
        state[...] = later_ref[...]

    cumul = cumul_ref[...]
    last = cumul[SPAN - 1 : SPAN, :]
    key_rows = key_ref[...]
    value_rows = value_ref[...]
    d_mixed = d_mixed_ref[...]
    before = saved_ref[0]
    d_after = state[...]
    up = jnp.exp(cumul)
    down = jnp.exp(-cumul)
    rest = jnp.exp(last - cumul)
    lifted = query_ref[...] * (HEAD_K ** (-0.5)) * up
    lowered = key_rows * down
    faded = key_rows * rest
    causal = triangle(False)
    scores = exact(lifted, lowered, contract_last) * causal
    d_scores = exact(d_mixed, value_rows, contract_last) * causal
    d_value = exact(scores, d_mixed, contract_rows) + exact(faded, d_after, contract_last)
    d_lifted = exact(d_scores, lowered, plain) + exact(d_mixed, before, plain)
    d_lowered = exact(d_scores, lifted, contract_rows)
    d_faded = exact(value_rows, d_after, plain)
    leak = d_faded * faded
    d_cumul = d_lifted * lifted - d_lowered * lowered - leak
    d_last = jnp.sum(leak, axis=0, keepdims=True) + jnp.exp(last) * jnp.sum(
        before * d_after, axis=0, keepdims=True
    )
    d_decay_ref[...] = exact(triangle(True), d_cumul, plain) + d_last
    grads_ref[:, :HEAD_K] = (d_lifted * up * (HEAD_K ** (-0.5))).astype(bf16)
    grads_ref[:, HEAD_K : 2 * HEAD_K] = (d_lowered * down + d_faded * rest).astype(bf16)
    grads_ref[:, 2 * HEAD_K : 2 * HEAD_K + HEAD_V] = d_value.astype(bf16)
    grads_ref[:, 2 * HEAD_K + HEAD_V :] = d_gate_ref[...]
    d_before = exact(d_mixed, lifted, contract_rows) + d_after * jnp.exp(last)
    state[...] = d_before * kept(resets, block)


def rows_of(width, column=0, backward=False):
    def place(step, order, resets):
        at = order.shape[0] - 1 - step if backward else step
        return (order[at], column)

    return pl.BlockSpec((SPAN, width), place)


def saved_of(backward=False):
    def place(step, order, resets):
        at = order.shape[0] - 1 - step if backward else step
        return (order[at], 0, 0)

    return pl.BlockSpec((1, HEAD_V, HEAD_K), place)


def whole_of(shape):
    return pl.BlockSpec(shape, lambda step, order, resets: (0,) * len(shape))


def over_blocks(kernel, order, resets, operands, in_specs, outs, out_specs, scratch, flops, moved):
    return pl.pallas_call(
        kernel,
        out_shape=outs,
        grid_spec=pltpu.PrefetchScalarGridSpec(
            num_scalar_prefetch=2,
            grid=(order.shape[0],),
            in_specs=in_specs,
            out_specs=out_specs,
            scratch_shapes=scratch,
        ),
        compiler_params=pltpu.CompilerParams(
            dimension_semantics=("arbitrary",), vmem_limit_bytes=40 << 20
        ),
        cost_estimate=pl.CostEstimate(flops=flops, bytes_accessed=moved, transcendentals=0),
    )(order, resets, *operands)


def shape_of(shape, dtype=f32):
    return jax.ShapeDtypeStruct(shape, dtype)


def swapped(value):
    return lax.ppermute(value, "c", [(0, 1), (1, 0)])


def neighbour(value, distance):
    return lax.ppermute(value, "t", [(i, i ^ distance) for i in range(GROUP)])


def plane_gather(value):
    arrived = [neighbour(value, distance) for distance in (3, 1, 2)]
    return jnp.concatenate([value, arrived[1], arrived[2], arrived[0]], axis=0)


def plane_sum(produce):
    arrived = [neighbour(produce(distance).astype(bf16), distance) for distance in (3, 1, 2)]
    total = produce(0)
    for part in arrived:
        total = total + part.astype(f32)
    return total


def deal_pairs(turn):
    pairs = []
    for t in range(GROUP):
        for c in range(2):
            pairs.append((t * 2 + c, (2 * c + (t + turn) % 2) * 2 + t // 2))
    return pairs


def local(
    layer_input, cotangent, teacher, target_slot, seq_start, seq_len,
    w_query, w_key, w_value, w_gate_out, w_out, w_ffn_gate, w_ffn_up, w_ffn_down,
    w_rank_down, w_rank_up, decay_bias, gain_attn, gain_ffn, gain_head,
):
    planes = lax.axis_size("o")
    devices = planes * GROUP
    o, t, c = (lax.axis_index("o"), lax.axis_index("t"), lax.axis_index("c"))
    even = t % 2 == 0
    _, rows, width = layer_input.shape
    shard = w_query.shape[0]
    rank = w_rank_down.shape[1]
    hidden_here = w_ffn_gate.shape[1] // 2
    tokens = GROUP * rows
    blocks = tokens // SPAN
    pair = 2 * rows // devices
    half = width // 2

    def mine(value):
        return lax.dynamic_index_in_dim(value, c, 0, keepdims=False)

    def arranged(value):
        shaped = value.reshape(value.shape[0], planes, 2, 2 * shard)
        return shaped.transpose(0, 2, 1, 3).reshape(value.shape)

    def restored(value):
        shaped = value.reshape(value.shape[0], 2, planes, 2 * shard)
        return shaped.transpose(0, 2, 1, 3).reshape(value.shape)

    def either(first, second):
        return (jnp.where(even, first, second), jnp.where(even, second, first))

    def fetch(first, second):
        sent = either(first, second)
        got = [lax.ppermute(sent[turn], ("t", "c"), deal_pairs(turn)) for turn in range(2)]
        return lax.all_gather(jnp.concatenate(either(*got), axis=0), ("c", "o"), axis=0, tiled=True)

    def deliver(left, right):
        theirs = lax.dynamic_slice_in_dim(left, (1 - c) * half, half, 1)
        ours = lax.dynamic_slice_in_dim(left, c * half, half, 1)
        arrived = swapped(outer_sum(theirs, right).astype(bf16))
        total = (outer_sum(ours, right) + arrived.astype(f32)).astype(bf16)
        part = lax.psum_scatter(total, "o", scatter_dimension=0, tiled=True)
        sent = either(part[:shard], part[shard:])
        got = [lax.ppermute(sent[turn], ("t", "c"), deal_pairs(turn)) for turn in range(2)]
        return [piece.astype(f32) for piece in either(*got)]

    targets = mine(target_slot)
    destination = targets // rows
    offset = targets % rows
    ids = jnp.arange(devices, dtype=jnp.int32)
    matches = (destination[:, None] == ids[None, :]).astype(bf16)
    index = jnp.arange(rows, dtype=jnp.int32)
    earlier = (index[:, None] > index[None, :]).astype(bf16)
    arrival = jnp.sum(project(earlier, matches) * matches.astype(f32), axis=1).astype(jnp.int32)
    slot = destination * pair + arrival
    pack = (jnp.arange(devices * pair, dtype=jnp.int32)[:, None] == slot[None, :]).astype(bf16)

    def exchange(value):
        return lax.all_to_all(value, ("o", "t"), split_axis=0, concat_axis=0, tiled=True)

    tag = jnp.pad((offset + 1).astype(bf16)[:, None], ((0, 0), (0, LANES - 1)))
    home_in = jnp.concatenate([arranged(mine(layer_input)), tag], axis=1)
    got_in = exchange(project(pack, home_in).astype(bf16))
    got_tag = got_in[:, width].astype(jnp.int32) - 1
    unpack = (got_tag[:, None] == index[None, :]).astype(bf16)
    layout_in = outer_sum(unpack, got_in[:, :width]).astype(bf16)
    got_grad = exchange(project(pack, arranged(mine(cotangent))).astype(bf16))
    layout_grad = outer_sum(unpack, got_grad).astype(bf16)

    def slice_of(weight, which):
        wide = weight.shape[1] // 2
        return weight[:, which * wide : (which + 1) * wide]

    extras = jnp.concatenate(
        [
            w_rank_down,
            gain_attn[:, None],
            gain_ffn[:, None],
            jnp.zeros((shard, LANES - rank - 2), bf16),
        ],
        axis=1,
    )
    first_pieces = [
        jnp.concatenate(
            [slice_of(w, which) for w in (w_query, w_key, w_value, w_gate_out)] + [extras], axis=1
        )
        for which in range(2)
    ]
    wide_first = first_pieces[0].shape[1] - LANES
    w_first = fetch(*first_pieces)
    wo = fetch(slice_of(w_out, 0), slice_of(w_out, 1))
    w_gate_up = fetch(
        *[
            jnp.concatenate([slice_of(w_ffn_gate, which), slice_of(w_ffn_up, which)], axis=1)
            for which in range(2)
        ]
    )
    w_down = fetch(slice_of(w_ffn_down, 0), slice_of(w_ffn_down, 1))
    rank_down = w_first[:, wide_first : wide_first + rank]
    gain_one = w_first[:, wide_first + rank].astype(f32)
    gain_two = w_first[:, wide_first + rank + 1].astype(f32)
    ranked = jnp.concatenate([w_rank_up, decay_bias[None, :]], axis=0)
    other_ranked = swapped(ranked)
    ranked = jnp.where(t // 2 == c, ranked, other_ranked).astype(f32)
    ranked = jnp.where(even, ranked[:, :HEAD_K], ranked[:, HEAD_K:])
    rank_up, bias = (ranked[:rank], ranked[rank])
    head_gain = gain_head.astype(f32)[None, :]

    starts, lengths = (mine(seq_start), mine(seq_len))
    own_positions = (o * GROUP + t) * rows + index
    own_valid = layout_valid(starts, lengths, own_positions)[:, None]
    block_ids = jnp.arange(blocks, dtype=jnp.int32)
    block_first = o * tokens + block_ids * SPAN
    resets = jnp.any(block_first[:, None] == starts[None, :], axis=1).astype(jnp.int32)
    per_member = rows // SPAN
    order = ((block_ids // per_member) ^ t) * per_member + block_ids % per_member

    inputs = layout_in.astype(f32)
    scale_one = rms_scale(inputs)
    unit_one = inputs * scale_one
    plane_in = plane_gather(layout_in).astype(f32)
    normed = (plane_in * rms_scale(plane_in) * gain_one).astype(bf16)
    upstream = layout_grad.astype(f32) * own_valid
    ffn_grad = plane_gather(upstream.astype(bf16))
    projected = project(normed, w_first)
    rank_rows = projected[:, wide_first : wide_first + rank]
    logits = jnp.dot(rank_rows, rank_up, precision=highest) + bias
    decays = jax.nn.log_sigmoid(logits) / 16.0
    state_shape = pltpu.VMEM((HEAD_V, HEAD_K), f32)
    through_shape = pltpu.VMEM((8, HEAD_K), f32)
    key_spec = functools.partial(rows_of, HEAD_K, 1)
    value_spec = functools.partial(rows_of, HEAD_V, 1)
    gate_spec = functools.partial(rows_of, HEAD_V, 2)
    narrow = functools.partial(rows_of, HEAD_K, 0)
    broad = functools.partial(rows_of, HEAD_V, 0)
    cumul, left = over_blocks(
        states_kernel, order, resets,
        (projected, projected, decays),
        [key_spec(), value_spec(), narrow()],
        (shape_of((tokens, HEAD_K)), shape_of((HEAD_V + 8, HEAD_K))),
        (narrow(), whole_of((HEAD_V + 8, HEAD_K))),
        [state_shape, through_shape],
        1 << 30, 6 << 20,
    )
    leaving, through = (left[:HEAD_V], left[HEAD_V : HEAD_V + 1])

    def shifted(value, distance):
        reach = planes - abs(distance)
        if distance > 0:
            hops = [(i, i + distance) for i in range(reach)]
        else:
            hops = [(i - distance, i) for i in range(reach)]
        return lax.ppermute(value, "o", hops)

    passed = [shifted(left, d) for d in range(1, planes)]
    entering = passed[-1][:HEAD_V]
    for d in range(planes - 2, 0, -1):
        entering = entering * passed[d - 1][HEAD_V : HEAD_V + 1] + passed[d - 1][:HEAD_V]
    gated, mixed, saved = over_blocks(
        mix_kernel, order, resets,
        (projected, projected, projected, projected, cumul, head_gain, entering),
        [narrow(), key_spec(), value_spec(), gate_spec(), narrow(), whole_of((1, HEAD_V)), whole_of((HEAD_V, HEAD_K))],
        (shape_of((tokens, HEAD_V), bf16), shape_of((tokens, HEAD_V)), shape_of((blocks, HEAD_V, HEAD_K))),
        (broad(), broad(), saved_of()),
        [state_shape],
        4 << 30, 16 << 20,
    )

    def member(value, distance):
        return value[distance * rows : (distance + 1) * rows]

    attended = plane_sum(lambda d: project_back(member(gated, d), wo))
    hidden = inputs + attended

    scale_two = rms_scale(hidden)
    unit_two = hidden * scale_two
    normed_two = plane_gather((unit_two * gain_two).astype(bf16))
    gate_up = project(normed_two, w_gate_up)
    gating, upward = (gate_up[:, :hidden_here], gate_up[:, hidden_here:])
    up_sig = jax.nn.sigmoid(gating)
    gate_silu = gating * up_sig
    product = (gate_silu * upward).astype(bf16)
    ffn_out = plane_sum(lambda d: project_back(member(product, d), w_down))
    result = ((hidden + ffn_out) * own_valid).astype(bf16)

    def homeward(value):
        back = exchange(project(unpack, value).astype(bf16))
        return restored(outer_sum(pack, back).astype(bf16))

    own_output = homeward(result)
    d_product = project(ffn_grad, w_down)
    d_gating = d_product * upward * up_sig * (1.0 + gating * (1.0 - up_sig))
    d_upward = d_product * gate_silu
    d_gate_up = jnp.concatenate([d_gating.astype(bf16), d_upward.astype(bf16)], axis=1)
    d_normed_two = plane_sum(lambda d: project_back(member(d_gate_up, d), w_gate_up))
    grad_down = deliver(ffn_grad, product)
    grad_gate_up = deliver(normed_two, d_gate_up)
    grad_gain_two = jnp.sum(d_normed_two * unit_two, axis=0)
    d_hidden = upstream + norm_back(d_normed_two * gain_two, unit_two, scale_two)

    attn_grad = plane_gather(d_hidden.astype(bf16))
    d_gated = project(attn_grad, wo)
    grad_out = deliver(attn_grad, gated)
    d_mixed, d_gate_pre, head_part, pulled = over_blocks(
        pull_kernel, order, resets,
        (projected, projected, cumul, mixed, d_gated, head_gain),
        [narrow(), gate_spec(), narrow(), broad(), broad(), whole_of((1, HEAD_V))],
        (
            shape_of((tokens, HEAD_V)),
            shape_of((tokens, HEAD_V), bf16),
            shape_of((8, HEAD_V)),
            shape_of((HEAD_V, HEAD_K)),
        ),
        (broad(), broad(), whole_of((8, HEAD_V)), whole_of((HEAD_V, HEAD_K))),
        [through_shape],
        1 << 30, 12 << 20,
    )
    pulled_ext = jnp.concatenate([pulled, left[HEAD_V:]], axis=0)
    returned = [shifted(pulled_ext, -d) for d in range(1, planes)]
    later = returned[-1][:HEAD_V]
    for d in range(planes - 2, 0, -1):
        later = later * returned[d - 1][HEAD_V : HEAD_V + 1] + returned[d - 1][:HEAD_V]
    flip = functools.partial
    grads, d_decays = over_blocks(
        back_kernel, order, resets,
        (projected, projected, projected, cumul, saved, d_mixed, d_gate_pre, later),
        [
            narrow(backward=True), key_spec(backward=True), value_spec(backward=True), narrow(backward=True),
            saved_of(True), broad(backward=True), broad(backward=True), whole_of((HEAD_V, HEAD_K)),
        ],
        (shape_of((tokens, wide_first), bf16), shape_of((tokens, HEAD_K))),
        (rows_of(wide_first, 0, True), narrow(backward=True)),
        [state_shape],
        8 << 30, 24 << 20,
    )
    d_logits = d_decays / 16.0 * jax.nn.sigmoid(-logits)
    grad_rank_up = lax.dot_general(rank_rows, d_logits, contract_rows, precision=highest)
    grad_bias = jnp.sum(d_logits, axis=0, keepdims=True)
    rank_part = lax.dot_general(d_logits, rank_up, contract_last, precision=highest)
    rank_part = jnp.pad(rank_part, ((0, 0), (0, LANES - rank)))

    def first_part(d):
        product_part = project_back(member(grads, d), w_first[:, :wide_first])
        return jnp.concatenate([product_part, member(rank_part, d)], axis=1)

    summed = plane_sum(first_part)
    grad_first = deliver(normed, grads)
    rank_grad = summed[:, width : width + rank].astype(bf16)
    d_normed = summed[:, :width] + project_back(rank_grad, rank_down)
    grad_gain_one = jnp.sum(d_normed * unit_one, axis=0)
    d_inputs = d_hidden + norm_back(d_normed * gain_one, unit_one, scale_one)
    own_input_grad = homeward(d_inputs.astype(bf16))
    own_normed = (unit_one * gain_one).astype(bf16)
    grad_rank_down = outer_sum(rank_grad, own_normed)

    home_valid = layout_valid(starts, lengths, targets)[:, None]
    difference = own_output.astype(f32) - mine(teacher).astype(f32)
    loss_part = jnp.sum(home_valid * difference * difference)
    small = jnp.concatenate([grad_rank_up, grad_bias], axis=0)
    member_ids = jnp.arange(GROUP, dtype=jnp.int32)[:, None, None]
    small = jnp.where(member_ids == t, small[None], 0.0).reshape(-1, HEAD_K)
    wide_rows = jnp.concatenate([grad_rank_down, grad_gain_one[None], grad_gain_two[None]], axis=0)
    everything = jnp.concatenate(
        [
            small,
            jnp.sum(head_part, axis=0).reshape(-1, HEAD_K),
            jnp.full((1, HEAD_K), loss_part, f32),
            wide_rows.reshape(-1, HEAD_K),
        ],
        axis=0,
    )
    everything = everything + swapped(everything)
    for distance in (1, 2):
        everything = everything + neighbour(everything, distance)
    distance = 1
    while distance < planes:
        hops = [(i, i ^ distance) for i in range(planes)]
        everything = everything + lax.ppermute(everything, "o", hops)
        distance *= 2
    used = GROUP * (rank + 1)
    summed_small = everything[:used].reshape(GROUP, rank + 1, HEAD_K)
    pair_small = lax.dynamic_slice_in_dim(summed_small, 2 * c, 2, 0)
    pair_small = jnp.concatenate([pair_small[0], pair_small[1]], axis=1)
    head_rows = HEAD_V // HEAD_K
    summed_head = everything[used : used + head_rows].reshape(-1)
    summed_loss = everything[used + head_rows, 0]
    wide_sum = everything[used + head_rows + 1 :].reshape(rank + 2, width)
    own_column = (t // 2) * half + (o * 2 + t % 2) * shard
    own_wide = lax.dynamic_slice_in_dim(wide_sum, own_column, shard, 1)
    loss = summed_loss / (jnp.sum(seq_len).astype(f32) * width)

    def both(value):
        other = swapped(value)
        return jnp.stack([jnp.where(c == 0, value, other), jnp.where(c == 0, other, value)])

    def columns(pair_of, start, size):
        return jnp.concatenate([piece[:, start : start + size] for piece in pair_of], axis=1)

    return (
        both(own_output),
        loss,
        both(own_input_grad),
        columns(grad_first, 0, HEAD_K),
        columns(grad_first, HEAD_K, HEAD_K),
        columns(grad_first, 2 * HEAD_K, HEAD_V),
        columns(grad_first, 2 * HEAD_K + HEAD_V, HEAD_V),
        columns(grad_out, 0, HEAD_V),
        columns(grad_gate_up, 0, hidden_here),
        columns(grad_gate_up, hidden_here, hidden_here),
        columns(grad_down, 0, hidden_here),
        own_wide[:rank].T,
        pair_small[:rank],
        pair_small[rank],
        own_wide[rank],
        own_wide[rank + 1],
        summed_head,
    )


def solution(mesh):
    seq = ("o", "t")
    count = mesh.devices.shape[0]
    split = Mesh(mesh.devices.reshape(count // GROUP, GROUP, 2), ("o", "t", "c"))
    tokens = P(None, seq, None)
    weight = P(seq, "c")
    placed = (
        (tokens, tokens, tokens, P(None, seq), P(), P())
        + (weight,) * 8
        + (P(seq, None), P(None, "c"), P("c"), P(seq), P(seq), P())
    )
    return jax.shard_map(
        local,
        mesh=split,
        in_specs=placed,
        out_specs=(tokens, P(), tokens)
        + (weight,) * 8
        + (P(seq, None), P(None, "c"), P("c"), P(seq), P(seq), P()),
        check_vma=False,
    )
```

```python
import functools

import jax
import jax.numpy as jnp
from jax import lax
from jax.experimental import pallas as pl
from jax.experimental.pallas import tpu as pltpu
from jax.sharding import Mesh
from jax.sharding import PartitionSpec as P

SPAN = 64
HEAD_K = 256
HEAD_V = 512
GROUP = 4
MEMBER = 256
LANES = 128

eps = 1e-06
highest = lax.Precision.HIGHEST
contract_last = (((1,), (1,)), ((), ()))
contract_rows = (((0,), (0,)), ((), ()))
bf16 = jnp.bfloat16
f32 = jnp.float32


def rms_scale(values):
    return lax.rsqrt(jnp.mean(values * values, axis=-1, keepdims=True) + eps)


def layout_valid(starts, lengths, positions):
    begun = (positions[:, None] >= starts[None, :]).astype(jnp.int32)
    owner = jnp.sum(begun, axis=1) - 1
    ids = jnp.arange(starts.shape[0], dtype=jnp.int32)
    picked = (owner[:, None] == ids[None, :]).astype(jnp.int32)
    own_start = jnp.sum(picked * starts[None, :], axis=1)
    own_length = jnp.sum(picked * lengths[None, :], axis=1)
    return (positions - own_start < own_length).astype(f32)


def project(left, right):
    return jnp.dot(left, right, preferred_element_type=f32)


def project_back(left, right):
    return lax.dot_general(left, right, contract_last, preferred_element_type=f32)


def outer_sum(left, right):
    return lax.dot_general(left, right, contract_rows, preferred_element_type=f32)


def norm_back(grad_unit, unit, scaling):
    return scaling * (grad_unit - unit * jnp.mean(grad_unit * unit, axis=-1, keepdims=True))


def exact(left, right, dims):
    return lax.dot_general(left, right, dims, precision=highest, preferred_element_type=f32)


def brief(left, right, dims):
    return lax.dot_general(left.astype(bf16), right.astype(bf16), dims, preferred_element_type=f32)


plain = (((1,), (0,)), ((), ()))


def triangle(upper, size=SPAN):
    row = lax.broadcasted_iota(jnp.int32, (size, size), 0)
    col = lax.broadcasted_iota(jnp.int32, (size, size), 1)
    causal = col >= row if upper else row >= col
    if size > SPAN:
        causal = causal & (row // SPAN == col // SPAN)
    return jnp.where(causal, 1.0, 0.0).astype(f32)


def kept(resets, block):
    return jnp.where(resets[block] == 1, 0.0, 1.0)


def spans(reverse=False):
    count = MEMBER // SPAN
    return range(count - 1, -1, -1) if reverse else range(count)


def part(index):
    return slice(index * SPAN, (index + 1) * SPAN)


def states_kernel(order, resets, key_ref, value_ref, decay_ref, cumul_ref, left_ref, state, through):
    member = pl.program_id(0)

    @pl.when(member == 0)
    def _():
        state[...] = jnp.zeros_like(state)
        through[...] = jnp.ones_like(through)

    cumul_all = exact(triangle(False, MEMBER), decay_ref[...], plain)
    cumul_ref[...] = cumul_all
    current = state[...]
    passing = through[...]
    for i in spans():
        cumul = cumul_all[part(i)]
        last = cumul[SPAN - 1 : SPAN, :]
        faded = key_ref[part(i), :] * jnp.exp(last - cumul)
        fade = jnp.exp(last) * kept(resets, member * (MEMBER // SPAN) + i)
        current = current * fade + brief(value_ref[part(i), :], faded, contract_rows)
        passing = passing * fade
    state[...] = current
    through[...] = passing

    @pl.when(member == pl.num_programs(0) - 1)
    def _():
        left_ref[:HEAD_V, :] = current
        left_ref[HEAD_V:, :] = passing


def mix_kernel(
    order, resets, query_ref, key_ref, value_ref, gate_ref, cumul_ref, gain_ref, enter_ref,
    gated_ref, mixed_ref, saved_ref, state,
):
    member = pl.program_id(0)

    @pl.when(member == 0)
    def _():
        state[...] = enter_ref[...]

    causal = triangle(False)
    current = state[...]
    for i in spans():
        cumul = cumul_ref[part(i), :]
        last = cumul[SPAN - 1 : SPAN, :]
        key_rows = key_ref[part(i), :]
        value_rows = value_ref[part(i), :]
        lifted = query_ref[part(i), :] * (HEAD_K ** (-0.5)) * jnp.exp(cumul)
        lowered = key_rows * jnp.exp(-cumul)
        before = current * kept(resets, member * (MEMBER // SPAN) + i)
        saved_ref[i] = before
        scores = brief(lifted, lowered, contract_last) * causal
        mixed = brief(scores, value_rows, plain) + brief(lifted, before, contract_last)
        mixed_ref[part(i), :] = mixed
        faded = key_rows * jnp.exp(last - cumul)
        current = before * jnp.exp(last) + brief(value_rows, faded, contract_rows)
        square = jnp.mean(mixed * mixed, axis=-1, keepdims=True)
        unit = mixed * lax.rsqrt(jnp.maximum(square, 1.0))
        gate = gate_ref[part(i), :]
        gated_ref[part(i), :] = (unit * gain_ref[...] * (gate * jax.nn.sigmoid(gate))).astype(bf16)
    state[...] = current


def pull_kernel(
    order, resets, query_ref, gate_ref, cumul_ref, mixed_ref, grad_ref, gain_ref,
    d_mixed_ref, d_gate_ref, head_ref, pulled_ref, through,
):
    member = pl.program_id(0)

    @pl.when(member == 0)
    def _():
        through[...] = jnp.ones_like(through)
        pulled_ref[...] = jnp.zeros_like(pulled_ref)
        head_ref[...] = jnp.zeros_like(head_ref)

    gain = gain_ref[...]
    passing = through[...]
    reach = []
    for i in spans():
        cumul = cumul_ref[part(i), :]
        mixed = mixed_ref[part(i), :]
        gate = gate_ref[part(i), :]
        grad = grad_ref[part(i), :]
        square = jnp.mean(mixed * mixed, axis=-1, keepdims=True)
        scale = lax.rsqrt(jnp.maximum(square, 1.0))
        free = jnp.where(square > 1.0, 1.0, 0.0)
        unit = mixed * scale
        sig = jax.nn.sigmoid(gate)
        d_head = grad * (gate * sig)
        d_gate_ref[part(i), :] = (grad * (unit * gain) * sig * (1.0 + gate * (1.0 - sig))).astype(bf16)
        head_ref[...] += jnp.sum((d_head * unit).reshape(SPAN // 8, 8, HEAD_V), axis=0)
        scaled = d_head * gain
        d_mixed = scale * (scaled - free * unit * jnp.mean(scaled * unit, axis=-1, keepdims=True))
        d_mixed_ref[part(i), :] = d_mixed
        opened = passing * kept(resets, member * (MEMBER // SPAN) + i)
        lifted = query_ref[part(i), :] * (HEAD_K ** (-0.5)) * jnp.exp(cumul)
        reach.append(lifted * opened[:1, :])
        passing = opened * jnp.exp(cumul[SPAN - 1 : SPAN, :])
    pulled_ref[...] += brief(d_mixed_ref[...], jnp.concatenate(reach, axis=0), contract_rows)
    through[...] = passing


def back_kernel(
    order, resets, query_ref, key_ref, value_ref, cumul_ref, saved_ref, d_mixed_ref, d_gate_ref, later_ref,
    grads_ref, d_decay_ref, state,
):
    step = pl.program_id(0)
    member = pl.num_programs(0) - 1 - step

    @pl.when(step == 0)
    def _():
        state[...] = later_ref[...]

    causal = triangle(False)
    d_after = state[...]
    for i in spans(True):
        cumul = cumul_ref[part(i), :]
        last = cumul[SPAN - 1 : SPAN, :]
        key_rows = key_ref[part(i), :]
        value_rows = value_ref[part(i), :]
        d_mixed = d_mixed_ref[part(i), :]
        before = saved_ref[i]
        up = jnp.exp(cumul)
        down = jnp.exp(-cumul)
        rest = jnp.exp(last - cumul)
        lifted = query_ref[part(i), :] * (HEAD_K ** (-0.5)) * up
        lowered = key_rows * down
        faded = key_rows * rest
        scores = brief(lifted, lowered, contract_last) * causal
        d_scores = brief(d_mixed, value_rows, contract_last) * causal
        d_value = brief(scores, d_mixed, contract_rows) + brief(faded, d_after, contract_last)
        d_lifted = brief(d_scores, lowered, plain) + brief(d_mixed, before, plain)
        d_lowered = brief(d_scores, lifted, contract_rows)
        d_faded = brief(value_rows, d_after, plain)
        leak = d_faded * faded
        d_cumul = d_lifted * lifted - d_lowered * lowered - leak
        d_last = jnp.sum(leak, axis=0, keepdims=True) + jnp.exp(last) * jnp.sum(
            before * d_after, axis=0, keepdims=True
        )
        d_decay_ref[part(i), :] = exact(triangle(True), d_cumul, plain) + d_last
        grads_ref[part(i), :HEAD_K] = (d_lifted * up * (HEAD_K ** (-0.5))).astype(bf16)
        grads_ref[part(i), HEAD_K : 2 * HEAD_K] = (d_lowered * down + d_faded * rest).astype(bf16)
        grads_ref[part(i), 2 * HEAD_K : 2 * HEAD_K + HEAD_V] = d_value.astype(bf16)
        grads_ref[part(i), 2 * HEAD_K + HEAD_V :] = d_gate_ref[part(i), :]
        d_before = brief(d_mixed, lifted, contract_rows) + d_after * jnp.exp(last)
        d_after = d_before * kept(resets, member * (MEMBER // SPAN) + i)
    state[...] = d_after


def deal_kernel(devices, per_device, spread, pieces, n_weights, n_shares, *refs):
    refs = list(refs)
    value_ref = refs.pop(0)
    block_ref = refs.pop(0) if spread else None
    weight_refs, refs = refs[:n_weights], refs[n_weights:]
    got_ref = refs.pop(0)
    plane_ref = refs.pop(0) if spread else None
    share_refs, refs = refs[:n_shares], refs[n_shares:]
    send_sem, arrive_sem, own_sem, give_sem, take_sem = refs[:5]
    o, t, c = (lax.axis_index("o"), lax.axis_index("t"), lax.axis_index("c"))
    me = o * GROUP + t
    shard = weight_refs[0].shape[0]
    mesh_ids = pl.DeviceIdType.MESH
    barrier = pltpu.get_barrier_semaphore()

    def place(turn):
        peer = lax.rem(me + turn, devices)
        return peer, (lax.div(peer, GROUP), lax.rem(peer, GROUP), c)

    def greet(turn, carry):
        _, there = place(turn)
        pl.semaphore_signal(barrier, inc=1, device_id=there, device_id_type=mesh_ids)
        return carry

    def parcel(turn):
        peer, there = place(turn)
        return pltpu.make_async_remote_copy(
            src_ref=value_ref.at[pl.ds(peer * per_device, per_device)],
            dst_ref=got_ref.at[pl.ds(me * per_device, per_device)],
            send_sem=send_sem.at[turn - 1],
            recv_sem=arrive_sem.at[turn - 1],
            device_id=there,
            device_id_type=mesh_ids,
        )

    def send(turn, carry):
        parcel(turn).start()
        return carry

    def receive(turn, carry):
        parcel(turn).wait()
        return carry

    def share(number, which, turn):
        weight, out, column, size = pieces[number]
        return (
            weight_refs[weight].at[:, pl.ds(which * size if weight_refs[weight].shape[1] > size else 0, size)],
            share_refs[out].at[pl.ds(turn * shard, shard), pl.ds(column, size)],
        )

    def given(number, which):
        source, target = share(number, which, lax.rem(t, 2))
        return pltpu.make_async_remote_copy(
            src_ref=source,
            dst_ref=target,
            send_sem=give_sem.at[which, number],
            recv_sem=take_sem.at[lax.rem(t, 2), number],
            device_id=(o, 2 * c + which, lax.div(t, 2)),
            device_id_type=mesh_ids,
        )

    def held(number, which):
        source, target = share(number, which, lax.rem(t, 2))
        return pltpu.make_async_copy(source, target, give_sem.at[which, number])

    def taken(number, turn):
        source, target = share(number, 0, turn)
        return pltpu.make_async_remote_copy(
            src_ref=source,
            dst_ref=target,
            send_sem=give_sem.at[0, number],
            recv_sem=take_sem.at[turn, number],
            device_id=(o, lax.rem(t + 1, GROUP), c),
            device_id_type=mesh_ids,
        )

    lax.fori_loop(1, devices, greet, 0)
    for turn in range(GROUP):
        there = (o, lax.rem(t + turn, GROUP), 1 - c)
        pl.semaphore_signal(barrier, inc=1, device_id=there, device_id_type=mesh_ids)
    pl.semaphore_wait(barrier, devices - 1 + GROUP)
    blocks = []
    if spread:
        out_sem, in_sem = refs[5:]
        mates = (t + 1 - 2 * lax.rem(t, 2), lax.rem(t + 2, GROUP), GROUP - 1 - t)
        for slot, mate in enumerate(mates):
            blocks.append(
                pltpu.make_async_remote_copy(
                    src_ref=block_ref,
                    dst_ref=plane_ref.at[slot],
                    send_sem=out_sem.at[slot],
                    recv_sem=in_sem.at[slot],
                    device_id=(o, mate, c),
                    device_id_type=mesh_ids,
                )
            )
            blocks[-1].start()
    lax.fori_loop(1, devices, send, 0)
    for which in range(2):
        own = t == 2 * c + which

        @pl.when(own)
        def _():
            for number in range(len(pieces)):
                held(number, which).start()

        @pl.when(jnp.logical_not(own))
        def _():
            for number in range(len(pieces)):
                given(number, which).start()

    rows = pl.ds(me * per_device, per_device)
    keep = pltpu.make_async_copy(value_ref.at[rows], got_ref.at[rows], own_sem)
    keep.start()
    keep.wait()
    for block in blocks:
        block.wait()
    for which in range(2):
        own = t == 2 * c + which

        @pl.when(own)
        def _():
            for number in range(len(pieces)):
                held(number, which).wait()

        @pl.when(jnp.logical_not(own))
        def _():
            for number in range(len(pieces)):
                given(number, which).wait_send()
                taken(number, which).wait_recv()

    lax.fori_loop(1, devices, receive, 0)


def deal(value, devices, weights, shares, pieces, block=None):
    spread = block is not None
    count = pltpu.SemaphoreType.DMA((devices - 1,))
    few = pltpu.SemaphoreType.DMA((GROUP - 1,))
    pairs = pltpu.SemaphoreType.DMA((2, len(pieces)))
    anywhere = pl.BlockSpec(memory_space=pl.ANY)
    inside = pl.BlockSpec(memory_space=pltpu.VMEM)
    outs = [jax.ShapeDtypeStruct(value.shape, value.dtype)]
    if spread:
        outs.append(jax.ShapeDtypeStruct((GROUP - 1,) + block.shape, block.dtype))
    outs += [jax.ShapeDtypeStruct((2 * weights[0].shape[0], size), bf16) for size in shares]
    kernel = functools.partial(
        deal_kernel, devices, value.shape[0] // devices, spread, pieces, len(weights), len(shares)
    )
    return pl.pallas_call(
        kernel,
        out_shape=outs,
        in_specs=[anywhere] * (2 if spread else 1) + [inside] * len(weights),
        out_specs=[anywhere] * len(outs),
        scratch_shapes=[count, count, pltpu.SemaphoreType.DMA, pairs, pairs]
        + ([few, few] if spread else []),
        compiler_params=pltpu.CompilerParams(
            collective_id=2 if spread else 1, has_side_effects=True, vmem_limit_bytes=24 << 20
        ),
        cost_estimate=pl.CostEstimate(flops=0, bytes_accessed=150 << 20, transcendentals=0),
    )(*([value, block] if spread else [value]), *weights)


def rows_of(width, column=0, backward=False):
    def place(step, order, resets):
        at = order.shape[0] - 1 - step if backward else step
        return (order[at], column)

    return pl.BlockSpec((MEMBER, width), place)


def saved_of(backward=False):
    def place(step, order, resets):
        at = order.shape[0] - 1 - step if backward else step
        return (order[at], 0, 0)

    return pl.BlockSpec((MEMBER // SPAN, HEAD_V, HEAD_K), place)


def whole_of(shape):
    return pl.BlockSpec(shape, lambda step, order, resets: (0,) * len(shape))


def over_blocks(kernel, order, resets, operands, in_specs, outs, out_specs, scratch, flops, moved):
    return pl.pallas_call(
        kernel,
        out_shape=outs,
        grid_spec=pltpu.PrefetchScalarGridSpec(
            num_scalar_prefetch=2,
            grid=(order.shape[0],),
            in_specs=in_specs,
            out_specs=out_specs,
            scratch_shapes=scratch,
        ),
        compiler_params=pltpu.CompilerParams(
            dimension_semantics=("arbitrary",), vmem_limit_bytes=40 << 20
        ),
        cost_estimate=pl.CostEstimate(flops=flops, bytes_accessed=moved, transcendentals=0),
    )(order, resets, *operands)


def shape_of(shape, dtype=f32):
    return jax.ShapeDtypeStruct(shape, dtype)


def swapped(value):
    return lax.ppermute(value, "c", [(0, 1), (1, 0)])


def neighbour(value, distance):
    return lax.ppermute(value, "t", [(i, i ^ distance) for i in range(GROUP)])


def plane_gather(value):
    middle = value.shape[0] // 2
    near = neighbour(value, 1)
    far = neighbour(value, 2)
    upper = neighbour(near[:middle], 2)
    lower = neighbour(far[middle:], 1)
    return jnp.concatenate([value, near, far, upper, lower], axis=0)


def plane_sum(produce, hold=None):
    across = produce(3, 4).astype(bf16)
    middle = across.shape[0] // 2
    upper = neighbour(across[:middle], 1)
    lower = neighbour(across[middle:], 2)
    sides = produce(1, 3)
    near, far = (sides[: 2 * middle], sides[2 * middle :])
    if hold is not None:
        upper, lower, hold = lax.optimization_barrier((upper, lower, hold))
    near_upper = neighbour(near[:middle].astype(bf16), 1)
    far_lower = neighbour(far[middle:].astype(bf16), 2)
    near_lower = neighbour((near[middle:] + lower.astype(f32)).astype(bf16), 1)
    far_upper = neighbour((far[:middle] + upper.astype(f32)).astype(bf16), 2)
    arrived_near = jnp.concatenate([near_upper, near_lower], axis=0)
    arrived_far = jnp.concatenate([far_upper, far_lower], axis=0)
    total = produce(0, 1) + arrived_near.astype(f32) + arrived_far.astype(f32)
    return total if hold is None else (total, hold)


def deal_pairs(turn):
    pairs = []
    for t in range(GROUP):
        for c in range(2):
            pairs.append((t * 2 + c, (2 * c + (t + turn) % 2) * 2 + t // 2))
    return pairs


def local(
    layer_input, cotangent, teacher, target_slot, seq_start, seq_len,
    w_query, w_key, w_value, w_gate_out, w_out, w_ffn_gate, w_ffn_up, w_ffn_down,
    w_rank_down, w_rank_up, decay_bias, gain_attn, gain_ffn, gain_head,
):
    planes = lax.axis_size("o")
    devices = planes * GROUP
    o, t, c = (lax.axis_index("o"), lax.axis_index("t"), lax.axis_index("c"))
    even = t % 2 == 0
    _, rows, width = layer_input.shape
    shard = w_query.shape[0]
    rank = w_rank_down.shape[1]
    hidden_here = w_ffn_gate.shape[1] // 2
    tokens = GROUP * rows
    blocks = tokens // SPAN
    pair = 2 * rows // devices
    half = width // 2

    def mine(value):
        return lax.dynamic_index_in_dim(value, c, 0, keepdims=False)

    def arranged(value):
        shaped = value.reshape(value.shape[0], planes, 2, 2 * shard)
        return shaped.transpose(0, 2, 1, 3).reshape(value.shape)

    def restored(value):
        shaped = value.reshape(value.shape[0], 2, planes, 2 * shard)
        return shaped.transpose(0, 2, 1, 3).reshape(value.shape)

    def either(first, second):
        return (jnp.where(even, first, second), jnp.where(even, second, first))

    def fetch(block):
        return lax.all_gather(block, ("c", "o"), axis=0, tiled=True)

    def over_cores(left, right):
        theirs = lax.dynamic_slice_in_dim(left, (1 - c) * half, half, 1)
        ours = lax.dynamic_slice_in_dim(left, c * half, half, 1)
        arrived = swapped(outer_sum(theirs, right).astype(bf16))
        return (outer_sum(ours, right) + arrived.astype(f32)).astype(bf16)

    def over_planes(total):
        return lax.psum_scatter(total, "o", scatter_dimension=0, tiled=True)

    def deliver(part_sum):
        sent = either(part_sum[:shard], part_sum[shard:])
        got = [lax.ppermute(sent[turn], ("t", "c"), deal_pairs(turn)) for turn in range(2)]
        return [piece.astype(f32) for piece in either(*got)]

    def own_columns(value):
        count = value.shape[0]

        def keep_half(array, axis, bit, pass_on):
            kept_half = lax.dynamic_index_in_dim(array, bit, axis, keepdims=False)
            given = lax.dynamic_index_in_dim(array, 1 - bit, axis, keepdims=False)
            return kept_half + pass_on(given)

        value = value.reshape(count, 2, planes, 2, shard)
        value = keep_half(value, 1, t // 2, lambda given: neighbour(given, 2))
        value = keep_half(value, 2, t % 2, lambda given: neighbour(given, 1))
        span = planes
        while span > 1:
            span //= 2
            hops = [(i, i ^ span) for i in range(planes)]
            value = value.reshape(count, 2, span, shard)
            value = keep_half(value, 1, (o // span) % 2, lambda given: lax.ppermute(given, "o", hops))
        value = value.reshape(count, shard)
        return value + swapped(value)

    targets = mine(target_slot)
    destination = targets // rows
    offset = targets % rows
    ids = jnp.arange(devices, dtype=jnp.int32)
    matches = (destination[:, None] == ids[None, :]).astype(bf16)
    index = jnp.arange(rows, dtype=jnp.int32)
    earlier = (index[:, None] > index[None, :]).astype(bf16)
    arrival = jnp.sum(project(earlier, matches) * matches.astype(f32), axis=1).astype(jnp.int32)
    slot = destination * pair + arrival
    pack = (jnp.arange(devices * pair, dtype=jnp.int32)[:, None] == slot[None, :]).astype(bf16)

    def exchange(value):
        return lax.all_to_all(value, ("o", "t"), split_axis=0, concat_axis=0, tiled=True)

    tag = jnp.pad((offset + 1).astype(bf16)[:, None], ((0, 0), (0, LANES - 1)))
    home_in = jnp.concatenate([arranged(mine(layer_input)), tag], axis=1)
    packed_in = project(pack, home_in).astype(bf16)

    extras = jnp.concatenate(
        [
            w_rank_down,
            gain_attn[:, None],
            gain_ffn[:, None],
            jnp.zeros((shard, LANES - rank - 2), bf16),
        ],
        axis=1,
    )
    wide_first = 2 * HEAD_K + 2 * HEAD_V
    got_in, first_block, out_block = deal(
        packed_in,
        devices,
        (w_query, w_key, w_value, w_gate_out, extras, w_out),
        (wide_first + LANES, HEAD_V),
        (
            (0, 0, 0, HEAD_K),
            (1, 0, HEAD_K, HEAD_K),
            (2, 0, 2 * HEAD_K, HEAD_V),
            (3, 0, 2 * HEAD_K + HEAD_V, HEAD_V),
            (4, 0, wide_first, LANES),
            (5, 1, 0, HEAD_V),
        ),
    )
    got_tag = got_in[:, width].astype(jnp.int32) - 1
    unpack = (got_tag[:, None] == index[None, :]).astype(bf16)
    layout_in = outer_sum(unpack, got_in[:, :width]).astype(bf16)
    packed_grad = project(pack, arranged(mine(cotangent))).astype(bf16)
    packed_grad, packed_in = lax.optimization_barrier((packed_grad, packed_in))
    got_grad, others, gate_up_block, down_block = deal(
        packed_grad,
        devices,
        (w_ffn_gate, w_ffn_up, w_ffn_down),
        (2 * hidden_here, hidden_here),
        ((0, 0, 0, hidden_here), (1, 0, hidden_here, hidden_here), (2, 1, 0, hidden_here)),
        layout_in,
    )
    w_first = fetch(first_block)
    wo = fetch(out_block)
    rank_down = w_first[:, wide_first : wide_first + rank]
    gain_one = w_first[:, wide_first + rank].astype(f32)
    gain_two = w_first[:, wide_first + rank + 1].astype(f32)
    ranked = jnp.concatenate([w_rank_up, decay_bias[None, :]], axis=0)
    other_ranked = swapped(ranked)
    ranked = jnp.where(t // 2 == c, ranked, other_ranked).astype(f32)
    ranked = jnp.where(even, ranked[:, :HEAD_K], ranked[:, HEAD_K:])
    rank_up, bias = (ranked[:rank], ranked[rank])
    head_gain = gain_head.astype(f32)[None, :]

    starts, lengths = (mine(seq_start), mine(seq_len))
    own_positions = (o * GROUP + t) * rows + index
    own_valid = layout_valid(starts, lengths, own_positions)[:, None]
    block_ids = jnp.arange(blocks, dtype=jnp.int32)
    block_first = o * tokens + block_ids * SPAN
    resets = jnp.any(block_first[:, None] == starts[None, :], axis=1).astype(jnp.int32)
    order = jnp.arange(GROUP, dtype=jnp.int32) ^ t

    inputs = layout_in.astype(f32)
    scale_one = rms_scale(inputs)
    unit_one = inputs * scale_one
    plane_in = jnp.concatenate([layout_in, others.reshape(-1, width)], axis=0).astype(f32)
    normed = (plane_in * rms_scale(plane_in) * gain_one).astype(bf16)
    projected = project(normed, w_first)
    rank_rows = projected[:, wide_first : wide_first + rank]
    logits = jnp.dot(rank_rows, rank_up, precision=highest) + bias
    decays = jax.nn.log_sigmoid(logits) / 16.0
    state_shape = pltpu.VMEM((HEAD_V, HEAD_K), f32)
    through_shape = pltpu.VMEM((8, HEAD_K), f32)
    key_spec = functools.partial(rows_of, HEAD_K, 1)
    value_spec = functools.partial(rows_of, HEAD_V, 1)
    gate_spec = functools.partial(rows_of, HEAD_V, 2)
    narrow = functools.partial(rows_of, HEAD_K, 0)
    broad = functools.partial(rows_of, HEAD_V, 0)
    projected, got_grad = lax.optimization_barrier((projected, got_grad))
    cumul, left = over_blocks(
        states_kernel, order, resets,
        (projected, projected, decays),
        [key_spec(), value_spec(), narrow()],
        (shape_of((tokens, HEAD_K)), shape_of((HEAD_V + 8, HEAD_K))),
        (narrow(), whole_of((HEAD_V + 8, HEAD_K))),
        [state_shape, through_shape],
        1 << 30, 6 << 20,
    )
    leaving, through = (left[:HEAD_V], left[HEAD_V : HEAD_V + 1])

    def shifted(value, distance):
        reach = planes - abs(distance)
        if distance > 0:
            hops = [(i, i + distance) for i in range(reach)]
        else:
            hops = [(i - distance, i) for i in range(reach)]
        return lax.ppermute(value, "o", hops)

    through_high = through.astype(bf16)
    through_low = (through - through_high.astype(f32)).astype(bf16)

    def carried(value, sign):
        packed = jnp.concatenate([value.astype(bf16), through_high, through_low], axis=0)
        passed = [shifted(packed, sign * d).astype(f32) for d in range(1, planes)]
        running = passed[-1][:HEAD_V]
        for nearer in passed[-2::-1]:
            running = running * (nearer[HEAD_V : HEAD_V + 1] + nearer[HEAD_V + 1 :]) + nearer[:HEAD_V]
        return running

    entering = carried(leaving, 1)
    layout_grad = outer_sum(unpack, got_grad).astype(bf16)
    upstream = layout_grad.astype(f32) * own_valid
    ffn_grad = plane_gather(upstream.astype(bf16))
    entering, ffn_grad, gate_up_block, down_block = lax.optimization_barrier(
        (entering, ffn_grad, gate_up_block, down_block)
    )
    w_gate_up = fetch(gate_up_block)
    w_down = fetch(down_block)
    gated, mixed, saved = over_blocks(
        mix_kernel, order, resets,
        (projected, projected, projected, projected, cumul, head_gain, entering),
        [narrow(), key_spec(), value_spec(), gate_spec(), narrow(), whole_of((1, HEAD_V)), whole_of((HEAD_V, HEAD_K))],
        (shape_of((tokens, HEAD_V), bf16), shape_of((tokens, HEAD_V)), shape_of((blocks, HEAD_V, HEAD_K))),
        (broad(), broad(), saved_of()),
        [state_shape],
        4 << 30, 16 << 20,
    )

    def members(value, first, last):
        return value[first * rows : last * rows]

    attended = plane_sum(lambda *d: project_back(members(gated, *d), wo))
    hidden = inputs + attended

    scale_two = rms_scale(hidden)
    unit_two = hidden * scale_two
    normed_two = plane_gather((unit_two * gain_two).astype(bf16))
    gate_up = project(normed_two, w_gate_up)
    gating, upward = (gate_up[:, :hidden_here], gate_up[:, hidden_here:])
    up_sig = jax.nn.sigmoid(gating)
    gate_silu = gating * up_sig
    product = (gate_silu * upward).astype(bf16)
    d_product = project(ffn_grad, w_down)
    d_gating = d_product * upward * up_sig * (1.0 + gating * (1.0 - up_sig))
    d_upward = d_product * gate_silu
    d_gate_up = jnp.concatenate([d_gating.astype(bf16), d_upward.astype(bf16)], axis=1)
    total_down = over_cores(ffn_grad, product)

    def second_part(*d):
        nonlocal total_down
        piece = project_back(members(d_gate_up, *d), w_gate_up)
        if d[0] == 1:
            piece, total_down = lax.optimization_barrier((piece, total_down))
        return piece

    d_normed_two = plane_sum(second_part)
    total_gate_up = over_cores(normed_two, d_gate_up)
    d_normed_two, total_gate_up = lax.optimization_barrier((d_normed_two, total_gate_up))
    part_down = over_planes(total_down)
    part_gate_up = over_planes(total_gate_up)
    grad_gain_two = jnp.sum(d_normed_two * unit_two, axis=0)
    d_hidden = upstream + norm_back(d_normed_two * gain_two, unit_two, scale_two)

    attn_grad = plane_gather(d_hidden.astype(bf16))
    attn_grad, part_down = lax.optimization_barrier((attn_grad, part_down))
    d_gated = project(attn_grad, wo)
    part_out = over_planes(over_cores(attn_grad, gated))
    product, d_gated = lax.optimization_barrier((product, d_gated))
    ffn_out = plane_sum(lambda *d: project_back(members(product, *d), w_down))
    result = ((hidden + ffn_out) * own_valid).astype(bf16)

    def both(value):
        other = swapped(value)
        return jnp.stack([jnp.where(c == 0, value, other), jnp.where(c == 0, other, value)])

    def outward(value):
        return exchange(project(unpack, value).astype(bf16))

    def homeward(value):
        return restored(outer_sum(pack, value).astype(bf16))

    d_mixed, d_gate_pre, head_part, pulled = over_blocks(
        pull_kernel, order, resets,
        (projected, projected, cumul, mixed, d_gated, head_gain),
        [narrow(), gate_spec(), narrow(), broad(), broad(), whole_of((1, HEAD_V))],
        (
            shape_of((tokens, HEAD_V)),
            shape_of((tokens, HEAD_V), bf16),
            shape_of((8, HEAD_V)),
            shape_of((HEAD_V, HEAD_K)),
        ),
        (broad(), broad(), whole_of((8, HEAD_V)), whole_of((HEAD_V, HEAD_K))),
        [through_shape],
        1 << 30, 12 << 20,
    )
    later = carried(pulled, -1)
    later, result, part_gate_up = lax.optimization_barrier((later, result, part_gate_up))
    back_output = outward(result)
    grads, d_decays = over_blocks(
        back_kernel, order, resets,
        (projected, projected, projected, cumul, saved, d_mixed, d_gate_pre, later),
        [
            narrow(backward=True), key_spec(backward=True), value_spec(backward=True), narrow(backward=True),
            saved_of(True), broad(backward=True), broad(backward=True), whole_of((HEAD_V, HEAD_K)),
        ],
        (shape_of((tokens, wide_first), bf16), shape_of((tokens, HEAD_K))),
        (rows_of(wide_first, 0, True), narrow(backward=True)),
        [state_shape],
        8 << 30, 24 << 20,
    )
    d_logits = d_decays / 16.0 * jax.nn.sigmoid(-logits)
    grad_rank_up = lax.dot_general(rank_rows, d_logits, contract_rows, precision=highest)
    grad_bias = jnp.sum(d_logits, axis=0, keepdims=True)
    rank_part = lax.dot_general(d_logits, rank_up, contract_last, precision=highest)
    rank_part = jnp.pad(rank_part, ((0, 0), (0, LANES - rank)))

    total_first = over_cores(normed, grads)

    def first_part(*d):
        nonlocal total_first
        product_part = project_back(members(grads, *d), w_first[:, :wide_first])
        piece = jnp.concatenate([product_part, members(rank_part, *d)], axis=1)
        if d[0] == 1:
            piece, total_first = lax.optimization_barrier((piece, total_first))
        return piece

    summed, back_output = plane_sum(first_part, back_output)
    part_first = over_planes(total_first)
    summed, part_out = lax.optimization_barrier((summed, part_out))
    own_output = homeward(back_output)
    both_output = both(own_output)
    grad_down = deliver(part_down)
    grad_gate_up = deliver(part_gate_up)
    grad_out = deliver(part_out)
    rank_grad = summed[:, width : width + rank].astype(bf16)
    d_normed = summed[:, :width] + project_back(rank_grad, rank_down)
    grad_gain_one = jnp.sum(d_normed * unit_one, axis=0)
    d_inputs = d_hidden + norm_back(d_normed * gain_one, unit_one, scale_one)
    back_input = outward(d_inputs.astype(bf16))
    own_normed = (unit_one * gain_one).astype(bf16)
    wide_rows = jnp.concatenate(
        [outer_sum(rank_grad, own_normed), grad_gain_one[None], grad_gain_two[None]], axis=0
    )
    own_wide = own_columns(wide_rows)

    home_valid = layout_valid(starts, lengths, targets)[:, None]
    difference = own_output.astype(f32) - mine(teacher).astype(f32)
    loss_part = jnp.sum(home_valid * difference * difference)
    small = jnp.concatenate([grad_rank_up, grad_bias], axis=0)
    member_ids = jnp.arange(GROUP, dtype=jnp.int32)[:, None, None]
    small = jnp.where(member_ids == t, small[None], 0.0).reshape(-1, HEAD_K)
    everything = jnp.concatenate(
        [
            small,
            jnp.sum(head_part, axis=0).reshape(-1, HEAD_K),
            jnp.full((1, HEAD_K), loss_part, f32),
        ],
        axis=0,
    )
    everything = everything + swapped(everything)
    for distance in (1, 2):
        everything = everything + neighbour(everything, distance)
    distance = 1
    while distance < planes:
        hops = [(i, i ^ distance) for i in range(planes)]
        everything = everything + lax.ppermute(everything, "o", hops)
        distance *= 2
    back_input, part_first, own_wide, everything, grad_down, grad_gate_up, grad_out, both_output = (
        lax.optimization_barrier(
            (back_input, part_first, own_wide, everything, grad_down, grad_gate_up, grad_out, both_output)
        )
    )
    used = GROUP * (rank + 1)
    summed_small = everything[:used].reshape(GROUP, rank + 1, HEAD_K)
    pair_small = lax.dynamic_slice_in_dim(summed_small, 2 * c, 2, 0)
    pair_small = jnp.concatenate([pair_small[0], pair_small[1]], axis=1)
    head_rows = HEAD_V // HEAD_K
    summed_head = everything[used : used + head_rows].reshape(-1)
    summed_loss = everything[used + head_rows, 0]
    own_input_grad = homeward(back_input)
    grad_first = deliver(part_first)
    loss = summed_loss / (jnp.sum(seq_len).astype(f32) * width)

    def columns(pair_of, start, size):
        return jnp.concatenate([piece[:, start : start + size] for piece in pair_of], axis=1)

    return (
        both_output,
        loss,
        both(own_input_grad),
        columns(grad_first, 0, HEAD_K),
        columns(grad_first, HEAD_K, HEAD_K),
        columns(grad_first, 2 * HEAD_K, HEAD_V),
        columns(grad_first, 2 * HEAD_K + HEAD_V, HEAD_V),
        columns(grad_out, 0, HEAD_V),
        columns(grad_gate_up, 0, hidden_here),
        columns(grad_gate_up, hidden_here, hidden_here),
        columns(grad_down, 0, hidden_here),
        own_wide[:rank].T,
        pair_small[:rank],
        pair_small[rank],
        own_wide[rank],
        own_wide[rank + 1],
        summed_head,
    )


def solution(mesh):
    seq = ("o", "t")
    count = mesh.devices.shape[0]
    split = Mesh(mesh.devices.reshape(count // GROUP, GROUP, 2), ("o", "t", "c"))
    tokens = P(None, seq, None)
    weight = P(seq, "c")
    placed = (
        (tokens, tokens, tokens, P(None, seq), P(), P())
        + (weight,) * 8
        + (P(seq, None), P(None, "c"), P("c"), P(seq), P(seq), P())
    )
    return jax.shard_map(
        local,
        mesh=split,
        in_specs=placed,
        out_specs=(tokens, P(), tokens)
        + (weight,) * 8
        + (P(seq, None), P(None, "c"), P("c"), P(seq), P(seq), P()),
        check_vma=False,
    )
```

```python
import functools

import jax
import jax.numpy as jnp
from jax import lax
from jax.experimental import pallas as pl
from jax.experimental.pallas import tpu as pltpu
from jax.sharding import Mesh
from jax.sharding import PartitionSpec as P

SPAN = 64
HEAD_K = 256
HEAD_V = 512
GROUP = 4
MEMBER = 256
LANES = 128

eps = 1e-06
highest = lax.Precision.HIGHEST
contract_last = (((1,), (1,)), ((), ()))
contract_rows = (((0,), (0,)), ((), ()))
bf16 = jnp.bfloat16
f32 = jnp.float32


def rms_scale(values):
    return lax.rsqrt(jnp.mean(values * values, axis=-1, keepdims=True) + eps)


def layout_valid(starts, lengths, positions):
    begun = (positions[:, None] >= starts[None, :]).astype(jnp.int32)
    owner = jnp.sum(begun, axis=1) - 1
    ids = jnp.arange(starts.shape[0], dtype=jnp.int32)
    picked = (owner[:, None] == ids[None, :]).astype(jnp.int32)
    own_start = jnp.sum(picked * starts[None, :], axis=1)
    own_length = jnp.sum(picked * lengths[None, :], axis=1)
    return (positions - own_start < own_length).astype(f32)


def project(left, right):
    return jnp.dot(left, right, preferred_element_type=f32)


def project_back(left, right):
    return lax.dot_general(left, right, contract_last, preferred_element_type=f32)


def outer_sum(left, right):
    return lax.dot_general(left, right, contract_rows, preferred_element_type=f32)


def norm_back(grad_unit, unit, scaling):
    return scaling * (grad_unit - unit * jnp.mean(grad_unit * unit, axis=-1, keepdims=True))


def exact(left, right, dims):
    return lax.dot_general(left, right, dims, precision=highest, preferred_element_type=f32)


def brief(left, right, dims):
    return lax.dot_general(left.astype(bf16), right.astype(bf16), dims, preferred_element_type=f32)


plain = (((1,), (0,)), ((), ()))


def triangle(upper, size=SPAN):
    row = lax.broadcasted_iota(jnp.int32, (size, size), 0)
    col = lax.broadcasted_iota(jnp.int32, (size, size), 1)
    causal = col >= row if upper else row >= col
    if size > SPAN:
        causal = causal & (row // SPAN == col // SPAN)
    return jnp.where(causal, 1.0, 0.0).astype(f32)


def kept(resets, block):
    return jnp.where(resets[block] == 1, 0.0, 1.0)


def spans(reverse=False):
    count = MEMBER // SPAN
    return range(count - 1, -1, -1) if reverse else range(count)


def part(index):
    return slice(index * SPAN, (index + 1) * SPAN)


def states_kernel(order, resets, key_ref, value_ref, decay_ref, cumul_ref, left_ref, state, through):
    member = pl.program_id(0)

    @pl.when(member == 0)
    def _():
        state[...] = jnp.zeros_like(state)
        through[...] = jnp.ones_like(through)

    cumul_all = exact(triangle(False, MEMBER), decay_ref[...], plain)
    cumul_ref[...] = cumul_all
    current = state[...]
    passing = through[...]
    for i in spans():
        cumul = cumul_all[part(i)]
        last = cumul[SPAN - 1 : SPAN, :]
        faded = key_ref[part(i), :] * jnp.exp(last - cumul)
        fade = jnp.exp(last) * kept(resets, member * (MEMBER // SPAN) + i)
        current = current * fade + brief(value_ref[part(i), :], faded, contract_rows)
        passing = passing * fade
    state[...] = current
    through[...] = passing

    @pl.when(member == pl.num_programs(0) - 1)
    def _():
        left_ref[:HEAD_V, :] = current
        left_ref[HEAD_V:, :] = passing


def mix_kernel(
    order, resets, query_ref, key_ref, value_ref, gate_ref, cumul_ref, gain_ref, enter_ref,
    gated_ref, mixed_ref, saved_ref, state,
):
    member = pl.program_id(0)

    @pl.when(member == 0)
    def _():
        state[...] = enter_ref[...]

    causal = triangle(False)
    current = state[...]
    for i in spans():
        cumul = cumul_ref[part(i), :]
        last = cumul[SPAN - 1 : SPAN, :]
        key_rows = key_ref[part(i), :]
        value_rows = value_ref[part(i), :]
        lifted = query_ref[part(i), :] * (HEAD_K ** (-0.5)) * jnp.exp(cumul)
        lowered = key_rows * jnp.exp(-cumul)
        before = current * kept(resets, member * (MEMBER // SPAN) + i)
        saved_ref[i] = before
        scores = brief(lifted, lowered, contract_last) * causal
        mixed = brief(scores, value_rows, plain) + brief(lifted, before, contract_last)
        mixed_ref[part(i), :] = mixed
        faded = key_rows * jnp.exp(last - cumul)
        current = before * jnp.exp(last) + brief(value_rows, faded, contract_rows)
        square = jnp.mean(mixed * mixed, axis=-1, keepdims=True)
        unit = mixed * lax.rsqrt(jnp.maximum(square, 1.0))
        gate = gate_ref[part(i), :]
        gated_ref[part(i), :] = (unit * gain_ref[...] * (gate * jax.nn.sigmoid(gate))).astype(bf16)
    state[...] = current


def pull_kernel(
    order, resets, query_ref, gate_ref, cumul_ref, mixed_ref, grad_ref, gain_ref,
    d_mixed_ref, d_gate_ref, head_ref, pulled_ref, through,
):
    member = pl.program_id(0)

    @pl.when(member == 0)
    def _():
        through[...] = jnp.ones_like(through)
        pulled_ref[...] = jnp.zeros_like(pulled_ref)
        head_ref[...] = jnp.zeros_like(head_ref)

    gain = gain_ref[...]
    passing = through[...]
    reach = []
    for i in spans():
        cumul = cumul_ref[part(i), :]
        mixed = mixed_ref[part(i), :]
        gate = gate_ref[part(i), :]
        grad = grad_ref[part(i), :]
        square = jnp.mean(mixed * mixed, axis=-1, keepdims=True)
        scale = lax.rsqrt(jnp.maximum(square, 1.0))
        free = jnp.where(square > 1.0, 1.0, 0.0)
        unit = mixed * scale
        sig = jax.nn.sigmoid(gate)
        d_head = grad * (gate * sig)
        d_gate_ref[part(i), :] = (grad * (unit * gain) * sig * (1.0 + gate * (1.0 - sig))).astype(bf16)
        head_ref[...] += jnp.sum((d_head * unit).reshape(SPAN // 8, 8, HEAD_V), axis=0)
        scaled = d_head * gain
        d_mixed = scale * (scaled - free * unit * jnp.mean(scaled * unit, axis=-1, keepdims=True))
        d_mixed_ref[part(i), :] = d_mixed
        opened = passing * kept(resets, member * (MEMBER // SPAN) + i)
        lifted = query_ref[part(i), :] * (HEAD_K ** (-0.5)) * jnp.exp(cumul)
        reach.append(lifted * opened[:1, :])
        passing = opened * jnp.exp(cumul[SPAN - 1 : SPAN, :])
    pulled_ref[...] += brief(d_mixed_ref[...], jnp.concatenate(reach, axis=0), contract_rows)
    through[...] = passing


def back_kernel(
    order, resets, query_ref, key_ref, value_ref, cumul_ref, saved_ref, d_mixed_ref, d_gate_ref, later_ref,
    grads_ref, d_decay_ref, state,
):
    step = pl.program_id(0)
    member = pl.num_programs(0) - 1 - step

    @pl.when(step == 0)
    def _():
        state[...] = later_ref[...]

    causal = triangle(False)
    d_after = state[...]
    for i in spans(True):
        cumul = cumul_ref[part(i), :]
        last = cumul[SPAN - 1 : SPAN, :]
        key_rows = key_ref[part(i), :]
        value_rows = value_ref[part(i), :]
        d_mixed = d_mixed_ref[part(i), :]
        before = saved_ref[i]
        up = jnp.exp(cumul)
        down = jnp.exp(-cumul)
        rest = jnp.exp(last - cumul)
        lifted = query_ref[part(i), :] * (HEAD_K ** (-0.5)) * up
        lowered = key_rows * down
        faded = key_rows * rest
        scores = brief(lifted, lowered, contract_last) * causal
        d_scores = brief(d_mixed, value_rows, contract_last) * causal
        d_value = brief(scores, d_mixed, contract_rows) + brief(faded, d_after, contract_last)
        d_lifted = brief(d_scores, lowered, plain) + brief(d_mixed, before, plain)
        d_lowered = brief(d_scores, lifted, contract_rows)
        d_faded = brief(value_rows, d_after, plain)
        leak = d_faded * faded
        d_cumul = d_lifted * lifted - d_lowered * lowered - leak
        d_last = jnp.sum(leak, axis=0, keepdims=True) + jnp.exp(last) * jnp.sum(
            before * d_after, axis=0, keepdims=True
        )
        d_decay_ref[part(i), :] = exact(triangle(True), d_cumul, plain) + d_last
        grads_ref[part(i), :HEAD_K] = (d_lifted * up * (HEAD_K ** (-0.5))).astype(bf16)
        grads_ref[part(i), HEAD_K : 2 * HEAD_K] = (d_lowered * down + d_faded * rest).astype(bf16)
        grads_ref[part(i), 2 * HEAD_K : 2 * HEAD_K + HEAD_V] = d_value.astype(bf16)
        grads_ref[part(i), 2 * HEAD_K + HEAD_V :] = d_gate_ref[part(i), :]
        d_before = brief(d_mixed, lifted, contract_rows) + d_after * jnp.exp(last)
        d_after = d_before * kept(resets, member * (MEMBER // SPAN) + i)
    state[...] = d_after


def deal_kernel(devices, per_device, spread, pieces, n_weights, n_shares, *refs):
    refs = list(refs)
    value_ref = refs.pop(0)
    block_ref = refs.pop(0) if spread else None
    weight_refs, refs = refs[:n_weights], refs[n_weights:]
    got_ref = refs.pop(0)
    plane_ref = refs.pop(0) if spread else None
    share_refs, refs = refs[:n_shares], refs[n_shares:]
    send_sem, arrive_sem, own_sem, give_sem, take_sem = refs[:5]
    o, t, c = (lax.axis_index("o"), lax.axis_index("t"), lax.axis_index("c"))
    me = o * GROUP + t
    shard = weight_refs[0].shape[0]
    mesh_ids = pl.DeviceIdType.MESH
    barrier = pltpu.get_barrier_semaphore()

    def place(turn):
        peer = lax.rem(me + turn, devices)
        return peer, (lax.div(peer, GROUP), lax.rem(peer, GROUP), c)

    def greet(turn, carry):
        _, there = place(turn)
        pl.semaphore_signal(barrier, inc=1, device_id=there, device_id_type=mesh_ids)
        return carry

    def parcel(turn):
        peer, there = place(turn)
        return pltpu.make_async_remote_copy(
            src_ref=value_ref.at[pl.ds(peer * per_device, per_device)],
            dst_ref=got_ref.at[pl.ds(me * per_device, per_device)],
            send_sem=send_sem.at[turn - 1],
            recv_sem=arrive_sem.at[turn - 1],
            device_id=there,
            device_id_type=mesh_ids,
        )

    def send(turn, carry):
        parcel(turn).start()
        return carry

    def receive(turn, carry):
        parcel(turn).wait()
        return carry

    def share(number, which, turn):
        weight, out, column, size = pieces[number]
        return (
            weight_refs[weight].at[:, pl.ds(which * size if weight_refs[weight].shape[1] > size else 0, size)],
            share_refs[out].at[pl.ds(turn * shard, shard), pl.ds(column, size)],
        )

    def given(number, which):
        source, target = share(number, which, lax.rem(t, 2))
        return pltpu.make_async_remote_copy(
            src_ref=source,
            dst_ref=target,
            send_sem=give_sem.at[which, number],
            recv_sem=take_sem.at[lax.rem(t, 2), number],
            device_id=(o, 2 * c + which, lax.div(t, 2)),
            device_id_type=mesh_ids,
        )

    def held(number, which):
        source, target = share(number, which, lax.rem(t, 2))
        return pltpu.make_async_copy(source, target, give_sem.at[which, number])

    def taken(number, turn):
        source, target = share(number, 0, turn)
        return pltpu.make_async_remote_copy(
            src_ref=source,
            dst_ref=target,
            send_sem=give_sem.at[0, number],
            recv_sem=take_sem.at[turn, number],
            device_id=(o, lax.rem(t + 1, GROUP), c),
            device_id_type=mesh_ids,
        )

    lax.fori_loop(1, devices, greet, 0)
    for turn in range(GROUP):
        there = (o, lax.rem(t + turn, GROUP), 1 - c)
        pl.semaphore_signal(barrier, inc=1, device_id=there, device_id_type=mesh_ids)
    pl.semaphore_wait(barrier, devices - 1 + GROUP)
    blocks = []
    if spread:
        out_sem, in_sem = refs[5:]
        mates = (t + 1 - 2 * lax.rem(t, 2), lax.rem(t + 2, GROUP), GROUP - 1 - t)
        for slot, mate in enumerate(mates):
            blocks.append(
                pltpu.make_async_remote_copy(
                    src_ref=block_ref,
                    dst_ref=plane_ref.at[slot],
                    send_sem=out_sem.at[slot],
                    recv_sem=in_sem.at[slot],
                    device_id=(o, mate, c),
                    device_id_type=mesh_ids,
                )
            )
            blocks[-1].start()
    lax.fori_loop(1, devices, send, 0)
    for which in range(2):
        own = t == 2 * c + which

        @pl.when(own)
        def _():
            for number in range(len(pieces)):
                held(number, which).start()

        @pl.when(jnp.logical_not(own))
        def _():
            for number in range(len(pieces)):
                given(number, which).start()

    rows = pl.ds(me * per_device, per_device)
    keep = pltpu.make_async_copy(value_ref.at[rows], got_ref.at[rows], own_sem)
    keep.start()
    keep.wait()
    for block in blocks:
        block.wait()
    for which in range(2):
        own = t == 2 * c + which

        @pl.when(own)
        def _():
            for number in range(len(pieces)):
                held(number, which).wait()

        @pl.when(jnp.logical_not(own))
        def _():
            for number in range(len(pieces)):
                given(number, which).wait_send()
                taken(number, which).wait_recv()

    lax.fori_loop(1, devices, receive, 0)


def deal(value, devices, weights, shares, pieces, block=None):
    spread = block is not None
    count = pltpu.SemaphoreType.DMA((devices - 1,))
    few = pltpu.SemaphoreType.DMA((GROUP - 1,))
    pairs = pltpu.SemaphoreType.DMA((2, len(pieces)))
    anywhere = pl.BlockSpec(memory_space=pl.ANY)
    inside = pl.BlockSpec(memory_space=pltpu.VMEM)
    outs = [jax.ShapeDtypeStruct(value.shape, value.dtype)]
    if spread:
        outs.append(jax.ShapeDtypeStruct((GROUP - 1,) + block.shape, block.dtype))
    outs += [jax.ShapeDtypeStruct((2 * weights[0].shape[0], size), bf16) for size in shares]
    kernel = functools.partial(
        deal_kernel, devices, value.shape[0] // devices, spread, pieces, len(weights), len(shares)
    )
    return pl.pallas_call(
        kernel,
        out_shape=outs,
        in_specs=[anywhere] * (2 if spread else 1) + [inside] * len(weights),
        out_specs=[anywhere] * len(outs),
        scratch_shapes=[count, count, pltpu.SemaphoreType.DMA, pairs, pairs]
        + ([few, few] if spread else []),
        compiler_params=pltpu.CompilerParams(
            collective_id=2 if spread else 1, has_side_effects=True, vmem_limit_bytes=24 << 20
        ),
        cost_estimate=pl.CostEstimate(flops=0, bytes_accessed=150 << 20, transcendentals=0),
    )(*([value, block] if spread else [value]), *weights)


def restore_kernel(planes, pack_ref, got_ref, out_ref):
    block = got_ref.shape[1] // (2 * planes)
    for number in range(2 * planes):
        r, o = (number // planes, number % planes)
        piece = lax.dot_general(
            pack_ref[...], got_ref[:, number * block : (number + 1) * block], contract_rows,
            preferred_element_type=f32,
        )
        at = (o * 2 + r) * block
        out_ref[:, at : at + block] = piece.astype(bf16)


def restore_rows(pack, got, planes):
    inside = pl.BlockSpec(memory_space=pltpu.VMEM)
    return pl.pallas_call(
        functools.partial(restore_kernel, planes),
        out_shape=jax.ShapeDtypeStruct((pack.shape[1], got.shape[1]), bf16),
        in_specs=[inside, inside],
        out_specs=inside,
        compiler_params=pltpu.CompilerParams(vmem_limit_bytes=24 << 20),
        cost_estimate=pl.CostEstimate(flops=1 << 29, bytes_accessed=4 << 20, transcendentals=0),
    )(pack, got)


def stack_kernel(core, own_ref, other_ref, out_ref):
    mine = pl.program_id(0) == core[0]

    @pl.when(mine)
    def _():
        out_ref[0] = own_ref[...]

    @pl.when(jnp.logical_not(mine))
    def _():
        out_ref[0] = other_ref[...]


def stack_cores(own, other, core):
    whole = pl.BlockSpec(own.shape, lambda step, core: (0, 0))
    return pl.pallas_call(
        stack_kernel,
        out_shape=jax.ShapeDtypeStruct((2,) + own.shape, own.dtype),
        grid_spec=pltpu.PrefetchScalarGridSpec(
            num_scalar_prefetch=1,
            grid=(2,),
            in_specs=[whole, whole],
            out_specs=pl.BlockSpec((1,) + own.shape, lambda step, core: (step, 0, 0)),
        ),
        compiler_params=pltpu.CompilerParams(vmem_limit_bytes=24 << 20),
        cost_estimate=pl.CostEstimate(flops=0, bytes_accessed=4 << 20, transcendentals=0),
    )(jnp.full((1,), core, jnp.int32), own, other)


def rows_of(width, column=0, backward=False):
    def place(step, order, resets):
        at = order.shape[0] - 1 - step if backward else step
        return (order[at], column)

    return pl.BlockSpec((MEMBER, width), place)


def saved_of(backward=False):
    def place(step, order, resets):
        at = order.shape[0] - 1 - step if backward else step
        return (order[at], 0, 0)

    return pl.BlockSpec((MEMBER // SPAN, HEAD_V, HEAD_K), place)


def whole_of(shape):
    return pl.BlockSpec(shape, lambda step, order, resets: (0,) * len(shape))


def over_blocks(kernel, order, resets, operands, in_specs, outs, out_specs, scratch, flops, moved):
    return pl.pallas_call(
        kernel,
        out_shape=outs,
        grid_spec=pltpu.PrefetchScalarGridSpec(
            num_scalar_prefetch=2,
            grid=(order.shape[0],),
            in_specs=in_specs,
            out_specs=out_specs,
            scratch_shapes=scratch,
        ),
        compiler_params=pltpu.CompilerParams(
            dimension_semantics=("arbitrary",), vmem_limit_bytes=40 << 20
        ),
        cost_estimate=pl.CostEstimate(flops=flops, bytes_accessed=moved, transcendentals=0),
    )(order, resets, *operands)


def shape_of(shape, dtype=f32):
    return jax.ShapeDtypeStruct(shape, dtype)


def swapped(value):
    return lax.ppermute(value, "c", [(0, 1), (1, 0)])


def neighbour(value, distance):
    return lax.ppermute(value, "t", [(i, i ^ distance) for i in range(GROUP)])


def plane_gather(value):
    middle = value.shape[0] // 2
    near = neighbour(value, 1)
    far = neighbour(value, 2)
    upper = neighbour(near[:middle], 2)
    lower = neighbour(far[middle:], 1)
    return jnp.concatenate([value, near, far, upper, lower], axis=0)


def plane_sum(produce, beside=None, early=None, hold=None):
    across = produce(3, 4).astype(bf16)
    middle = across.shape[0] // 2
    upper = neighbour(across[:middle], 1)
    lower = neighbour(across[middle:], 2)
    sides = produce(1, 3)
    near, far = (sides[: 2 * middle], sides[2 * middle :])
    own, beside = lax.optimization_barrier((produce(0, 1), beside))
    own, upper, lower, early = lax.optimization_barrier((own, upper, lower, early))
    near_upper = neighbour(near[:middle].astype(bf16), 1)
    far_lower = neighbour(far[middle:].astype(bf16), 2)
    near_lower = neighbour((near[middle:] + lower.astype(f32)).astype(bf16), 1)
    far_upper = neighbour((far[:middle] + upper.astype(f32)).astype(bf16), 2)
    arrived_near = jnp.concatenate([near_upper, near_lower], axis=0)
    arrived_far = jnp.concatenate([far_upper, far_lower], axis=0)
    if hold is not None:
        arrived_near, arrived_far, hold = lax.optimization_barrier((arrived_near, arrived_far, hold))
    total = own + arrived_near.astype(f32) + arrived_far.astype(f32)
    return total if hold is None else (total, beside, early, hold)


def deal_pairs(turn):
    pairs = []
    for t in range(GROUP):
        for c in range(2):
            pairs.append((t * 2 + c, (2 * c + (t + turn) % 2) * 2 + t // 2))
    return pairs


def local(
    layer_input, cotangent, teacher, target_slot, seq_start, seq_len,
    w_query, w_key, w_value, w_gate_out, w_out, w_ffn_gate, w_ffn_up, w_ffn_down,
    w_rank_down, w_rank_up, decay_bias, gain_attn, gain_ffn, gain_head,
):
    planes = lax.axis_size("o")
    devices = planes * GROUP
    o, t, c = (lax.axis_index("o"), lax.axis_index("t"), lax.axis_index("c"))
    even = t % 2 == 0
    _, rows, width = layer_input.shape
    shard = w_query.shape[0]
    rank = w_rank_down.shape[1]
    hidden_here = w_ffn_gate.shape[1] // 2
    tokens = GROUP * rows
    blocks = tokens // SPAN
    pair = 2 * rows // devices
    half = width // 2

    def mine(value):
        return lax.dynamic_index_in_dim(value, c, 0, keepdims=False)

    def arranged(value):
        shaped = value.reshape(value.shape[0], planes, 2, 2 * shard)
        return shaped.transpose(0, 2, 1, 3).reshape(value.shape)

    def either(first, second):
        return (jnp.where(even, first, second), jnp.where(even, second, first))

    def fetch(block):
        return lax.all_gather(block, ("c", "o"), axis=0, tiled=True)

    def over_cores(left, right):
        theirs = lax.dynamic_slice_in_dim(left, (1 - c) * half, half, 1)
        ours = lax.dynamic_slice_in_dim(left, c * half, half, 1)
        arrived = swapped(outer_sum(theirs, right).astype(bf16))
        return (outer_sum(ours, right) + arrived.astype(f32)).astype(bf16)

    def over_planes(total):
        return lax.psum_scatter(total, "o", scatter_dimension=0, tiled=True)

    def deliver(part_sum):
        sent = either(part_sum[:shard], part_sum[shard:])
        got = [lax.ppermute(sent[turn], ("t", "c"), deal_pairs(turn)) for turn in range(2)]
        return [piece.astype(f32) for piece in either(*got)]

    targets = mine(target_slot)
    destination = targets // rows
    offset = targets % rows
    ids = jnp.arange(devices, dtype=jnp.int32)
    matches = (destination[:, None] == ids[None, :]).astype(bf16)
    index = jnp.arange(rows, dtype=jnp.int32)
    earlier = (index[:, None] > index[None, :]).astype(bf16)
    arrival = jnp.sum(project(earlier, matches) * matches.astype(f32), axis=1).astype(jnp.int32)
    slot = destination * pair + arrival
    pack = (jnp.arange(devices * pair, dtype=jnp.int32)[:, None] == slot[None, :]).astype(bf16)

    def exchange(value):
        return lax.all_to_all(value, ("o", "t"), split_axis=0, concat_axis=0, tiled=True)

    tag = jnp.pad((offset + 1).astype(bf16)[:, None], ((0, 0), (0, LANES - 1)))
    home_in = jnp.concatenate([arranged(mine(layer_input)), tag], axis=1)
    packed_in = project(pack, home_in).astype(bf16)

    extras = jnp.concatenate(
        [
            w_rank_down,
            gain_attn[:, None],
            gain_ffn[:, None],
            jnp.zeros((shard, LANES - rank - 2), bf16),
        ],
        axis=1,
    )
    wide_first = 2 * HEAD_K + 2 * HEAD_V
    got_in, first_block, out_block = deal(
        packed_in,
        devices,
        (w_query, w_key, w_value, w_gate_out, extras, w_out),
        (wide_first + LANES, HEAD_V),
        (
            (0, 0, 0, HEAD_K),
            (1, 0, HEAD_K, HEAD_K),
            (2, 0, 2 * HEAD_K, HEAD_V),
            (3, 0, 2 * HEAD_K + HEAD_V, HEAD_V),
            (4, 0, wide_first, LANES),
            (5, 1, 0, HEAD_V),
        ),
    )
    got_tag = got_in[:, width].astype(jnp.int32) - 1
    unpack = (got_tag[:, None] == index[None, :]).astype(bf16)
    layout_in = outer_sum(unpack, got_in[:, :width]).astype(bf16)
    packed_grad = project(pack, arranged(mine(cotangent))).astype(bf16)
    packed_grad, packed_in = lax.optimization_barrier((packed_grad, packed_in))
    got_grad, others, gate_up_block, down_block = deal(
        packed_grad,
        devices,
        (w_ffn_gate, w_ffn_up, w_ffn_down),
        (2 * hidden_here, hidden_here),
        ((0, 0, 0, hidden_here), (1, 0, hidden_here, hidden_here), (2, 1, 0, hidden_here)),
        layout_in,
    )
    w_first = fetch(first_block)
    wo = fetch(out_block)
    w_gate_up = fetch(gate_up_block)
    w_down = fetch(down_block)
    rank_down = w_first[:, wide_first : wide_first + rank]
    gain_one = w_first[:, wide_first + rank].astype(f32)
    gain_two = w_first[:, wide_first + rank + 1].astype(f32)
    ranked = jnp.concatenate([w_rank_up, decay_bias[None, :]], axis=0)
    other_ranked = swapped(ranked)
    ranked = jnp.where(t // 2 == c, ranked, other_ranked).astype(f32)
    ranked = jnp.where(even, ranked[:, :HEAD_K], ranked[:, HEAD_K:])
    rank_up, bias = (ranked[:rank], ranked[rank])
    head_gain = gain_head.astype(f32)[None, :]

    starts, lengths = (mine(seq_start), mine(seq_len))
    own_positions = (o * GROUP + t) * rows + index
    own_valid = layout_valid(starts, lengths, own_positions)[:, None]
    block_ids = jnp.arange(blocks, dtype=jnp.int32)
    block_first = o * tokens + block_ids * SPAN
    resets = jnp.any(block_first[:, None] == starts[None, :], axis=1).astype(jnp.int32)
    order = jnp.arange(GROUP, dtype=jnp.int32) ^ t

    inputs = layout_in.astype(f32)
    scale_one = rms_scale(inputs)
    unit_one = inputs * scale_one
    plane_in = jnp.concatenate([layout_in, others.reshape(-1, width)], axis=0).astype(f32)
    normed = (plane_in * rms_scale(plane_in) * gain_one).astype(bf16)
    projected = project(normed, w_first)
    rank_rows = projected[:, wide_first : wide_first + rank]
    logits = jnp.dot(rank_rows, rank_up, precision=highest) + bias
    decays = jax.nn.log_sigmoid(logits) / 16.0
    state_shape = pltpu.VMEM((HEAD_V, HEAD_K), f32)
    through_shape = pltpu.VMEM((8, HEAD_K), f32)
    key_spec = functools.partial(rows_of, HEAD_K, 1)
    value_spec = functools.partial(rows_of, HEAD_V, 1)
    gate_spec = functools.partial(rows_of, HEAD_V, 2)
    narrow = functools.partial(rows_of, HEAD_K, 0)
    broad = functools.partial(rows_of, HEAD_V, 0)
    projected, got_grad = lax.optimization_barrier((projected, got_grad))
    cumul, left = over_blocks(
        states_kernel, order, resets,
        (projected, projected, decays),
        [key_spec(), value_spec(), narrow()],
        (shape_of((tokens, HEAD_K)), shape_of((HEAD_V + 8, HEAD_K))),
        (narrow(), whole_of((HEAD_V + 8, HEAD_K))),
        [state_shape, through_shape],
        1 << 30, 6 << 20,
    )
    leaving, through = (left[:HEAD_V], left[HEAD_V : HEAD_V + 1])

    def shifted(value, distance):
        reach = planes - abs(distance)
        if distance > 0:
            hops = [(i, i + distance) for i in range(reach)]
        else:
            hops = [(i - distance, i) for i in range(reach)]
        return lax.ppermute(value, "o", hops)

    through_high = through.astype(bf16)
    through_low = (through - through_high.astype(f32)).astype(bf16)

    def carried(value, sign):
        packed = jnp.concatenate([value.astype(bf16), through_high, through_low], axis=0)
        passed = [shifted(packed, sign * d).astype(f32) for d in range(1, planes)]
        running = passed[-1][:HEAD_V]
        for nearer in passed[-2::-1]:
            running = running * (nearer[HEAD_V : HEAD_V + 1] + nearer[HEAD_V + 1 :]) + nearer[:HEAD_V]
        return running

    entering = carried(leaving, 1)
    layout_grad = outer_sum(unpack, got_grad).astype(bf16)
    upstream = layout_grad.astype(f32) * own_valid
    own_grad = upstream.astype(bf16)
    ffn_grad = jnp.concatenate([own_grad] + [neighbour(own_grad, d) for d in (1, 2, 3)], axis=0)
    gated, mixed, saved = over_blocks(
        mix_kernel, order, resets,
        (projected, projected, projected, projected, cumul, head_gain, entering),
        [narrow(), key_spec(), value_spec(), gate_spec(), narrow(), whole_of((1, HEAD_V)), whole_of((HEAD_V, HEAD_K))],
        (shape_of((tokens, HEAD_V), bf16), shape_of((tokens, HEAD_V)), shape_of((blocks, HEAD_V, HEAD_K))),
        (broad(), broad(), saved_of()),
        [state_shape],
        4 << 30, 16 << 20,
    )

    def members(value, first, last):
        return value[first * rows : last * rows]

    attended = plane_sum(lambda *d: project_back(members(gated, *d), wo))
    attended, ffn_grad = lax.optimization_barrier((attended, ffn_grad))
    hidden = inputs + attended

    scale_two = rms_scale(hidden)
    unit_two = hidden * scale_two
    normed_two = plane_gather((unit_two * gain_two).astype(bf16))
    gate_up = project(normed_two, w_gate_up)
    gating, upward = (gate_up[:, :hidden_here], gate_up[:, hidden_here:])
    up_sig = jax.nn.sigmoid(gating)
    gate_silu = gating * up_sig
    product = (gate_silu * upward).astype(bf16)
    product, gating, upward = lax.optimization_barrier((product, gating, upward))
    up_sig = jax.nn.sigmoid(gating)
    gate_silu = gating * up_sig
    total_down = over_cores(ffn_grad, product)
    total_down, w_down = lax.optimization_barrier((total_down, w_down))
    d_product = project(ffn_grad, w_down)
    d_gating = d_product * upward * up_sig * (1.0 + gating * (1.0 - up_sig))
    d_upward = d_product * gate_silu
    d_gate_up = jnp.concatenate([d_gating.astype(bf16), d_upward.astype(bf16)], axis=1)

    def second_part(*d):
        return project_back(members(d_gate_up, *d), w_gate_up)

    part_down = over_planes(total_down)
    d_normed_two, total_gate_up, _, part_down = plane_sum(
        second_part, over_cores(normed_two, d_gate_up), hold=part_down
    )
    part_gate_up = over_planes(total_gate_up)
    grad_gain_two = jnp.sum(d_normed_two * unit_two, axis=0)
    d_hidden = upstream + norm_back(d_normed_two * gain_two, unit_two, scale_two)

    low_hidden, product = lax.optimization_barrier((d_hidden.astype(bf16), product))
    attn_grad = plane_gather(low_hidden)
    out_across = project_back(members(product, 3, 4), w_down).astype(bf16)
    out_sides = project_back(members(product, 1, 3), w_down).astype(bf16)
    out_own = project_back(members(product, 0, 1), w_down)
    attn_grad, out_across, out_sides, out_own = lax.optimization_barrier(
        (attn_grad, out_across, out_sides, out_own)
    )
    out_parts = [
        neighbour(out_sides[:rows], 1), neighbour(out_sides[rows:], 2), neighbour(out_across, 3)
    ]
    d_gated = project(attn_grad, wo)
    part_out = over_planes(over_cores(attn_grad, gated))

    def both(value):
        return stack_cores(value, swapped(value), c)

    def outward(value):
        return exchange(project(unpack, value).astype(bf16))

    def homeward(value):
        return restore_rows(pack, value, planes)

    d_mixed, d_gate_pre, head_part, pulled = over_blocks(
        pull_kernel, order, resets,
        (projected, projected, cumul, mixed, d_gated, head_gain),
        [narrow(), gate_spec(), narrow(), broad(), broad(), whole_of((1, HEAD_V))],
        (
            shape_of((tokens, HEAD_V)),
            shape_of((tokens, HEAD_V), bf16),
            shape_of((8, HEAD_V)),
            shape_of((HEAD_V, HEAD_K)),
        ),
        (broad(), broad(), whole_of((8, HEAD_V)), whole_of((HEAD_V, HEAD_K))),
        [through_shape],
        1 << 30, 12 << 20,
    )
    later = carried(pulled, -1)
    later, out_sides, out_across, out_own, part_gate_up = lax.optimization_barrier(
        (later, out_sides, out_across, out_own, part_gate_up)
    )
    for piece in out_parts:
        out_own = out_own + piece.astype(f32)
    result = ((hidden + out_own) * own_valid).astype(bf16)
    back_output = outward(result)
    grads, d_decays = over_blocks(
        back_kernel, order, resets,
        (projected, projected, projected, cumul, saved, d_mixed, d_gate_pre, later),
        [
            narrow(backward=True), key_spec(backward=True), value_spec(backward=True), narrow(backward=True),
            saved_of(True), broad(backward=True), broad(backward=True), whole_of((HEAD_V, HEAD_K)),
        ],
        (shape_of((tokens, wide_first), bf16), shape_of((tokens, HEAD_K))),
        (rows_of(wide_first, 0, True), narrow(backward=True)),
        [state_shape],
        8 << 30, 24 << 20,
    )
    d_logits = d_decays / 16.0 * jax.nn.sigmoid(-logits)
    grad_rank_up = lax.dot_general(rank_rows, d_logits, contract_rows, precision=highest)
    grad_bias = jnp.sum(d_logits, axis=0, keepdims=True)
    rank_part = lax.dot_general(d_logits, rank_up, contract_last, precision=highest)
    rank_part = jnp.pad(rank_part, ((0, 0), (0, LANES - rank)))

    total_first = over_cores(normed, grads)

    def first_part(*d):
        product_part = project_back(members(grads, *d), w_first[:, :wide_first])
        return jnp.concatenate([product_part, members(rank_part, *d)], axis=1)

    summed, total_first, back_output, _ = plane_sum(first_part, total_first, back_output, d_hidden)
    part_first = over_planes(total_first)
    own_output = homeward(back_output)
    both_output = both(own_output)
    rank_grad = summed[:, width : width + rank].astype(bf16)
    d_normed = summed[:, :width] + project_back(rank_grad, rank_down)
    grad_gain_one = jnp.sum(d_normed * unit_one, axis=0)
    d_inputs = d_hidden + norm_back(d_normed * gain_one, unit_one, scale_one)
    packed_input = project(unpack, d_inputs.astype(bf16)).astype(bf16)
    own_normed = (unit_one * gain_one).astype(bf16)
    wide_rows = jnp.concatenate(
        [outer_sum(rank_grad, own_normed), grad_gain_one[None], grad_gain_two[None]], axis=0
    )

    home_valid = layout_valid(starts, lengths, targets)[:, None]
    difference = own_output.astype(f32) - mine(teacher).astype(f32)
    loss_part = jnp.sum(home_valid * difference * difference)
    small = jnp.concatenate([grad_rank_up, grad_bias], axis=0)
    member_ids = jnp.arange(GROUP, dtype=jnp.int32)[:, None, None]
    small = jnp.where(member_ids == t, small[None], 0.0).reshape(-1, HEAD_K)
    everything = jnp.concatenate(
        [
            small,
            jnp.sum(head_part, axis=0).reshape(-1, HEAD_K),
            jnp.full((1, HEAD_K), loss_part, f32),
        ],
        axis=0,
    )
    packed_input, everything = lax.optimization_barrier((packed_input, everything))
    back_input = exchange(packed_input)
    everything = jnp.concatenate([everything, wide_rows.reshape(-1, HEAD_K)], axis=0)
    everything = everything + swapped(everything)
    everything, part_down, part_gate_up, part_out = lax.optimization_barrier(
        (everything, part_down, part_gate_up, part_out)
    )
    grad_down = deliver(part_down)
    grad_gate_up = deliver(part_gate_up)
    grad_out = deliver(part_out)
    for distance in (1, 2):
        everything = everything + neighbour(everything, distance)
    distance = 1
    while distance < planes:
        hops = [(i, i ^ distance) for i in range(planes)]
        everything = everything + lax.ppermute(everything, "o", hops)
        distance *= 2
    def columns(pair_of, start, size):
        return jnp.concatenate([piece[:, start : start + size] for piece in pair_of], axis=1)

    grad_first = deliver(part_first)
    finished = (
        columns(grad_first, 0, HEAD_K),
        columns(grad_first, HEAD_K, HEAD_K),
        columns(grad_first, 2 * HEAD_K, HEAD_V),
        columns(grad_first, 2 * HEAD_K + HEAD_V, HEAD_V),
        columns(grad_out, 0, HEAD_V),
        columns(grad_gate_up, 0, hidden_here),
        columns(grad_gate_up, hidden_here, hidden_here),
        columns(grad_down, 0, hidden_here),
    )
    back_input, finished, everything, both_output = lax.optimization_barrier(
        (back_input, finished, everything, both_output)
    )
    own_column = (t // 2) * half + (o * 2 + t % 2) * shard
    wide_sum = everything[GROUP * (rank + 1) + HEAD_V // HEAD_K + 1 :].reshape(rank + 2, width)
    own_wide = lax.dynamic_slice_in_dim(wide_sum, own_column, shard, 1)
    used = GROUP * (rank + 1)
    summed_small = everything[:used].reshape(GROUP, rank + 1, HEAD_K)
    pair_small = lax.dynamic_slice_in_dim(summed_small, 2 * c, 2, 0)
    pair_small = jnp.concatenate([pair_small[0], pair_small[1]], axis=1)
    head_rows = HEAD_V // HEAD_K
    summed_head = everything[used : used + head_rows].reshape(-1)
    summed_loss = everything[used + head_rows, 0]
    own_input_grad = homeward(back_input)
    loss = summed_loss / (jnp.sum(seq_len).astype(f32) * width)

    return (
        both_output,
        loss,
        both(own_input_grad),
        *finished,
        own_wide[:rank].T,
        pair_small[:rank],
        pair_small[rank],
        own_wide[rank],
        own_wide[rank + 1],
        summed_head,
    )


def solution(mesh):
    seq = ("o", "t")
    count = mesh.devices.shape[0]
    split = Mesh(mesh.devices.reshape(count // GROUP, GROUP, 2), ("o", "t", "c"))
    tokens = P(None, seq, None)
    weight = P(seq, "c")
    placed = (
        (tokens, tokens, tokens, P(None, seq), P(), P())
        + (weight,) * 8
        + (P(seq, None), P(None, "c"), P("c"), P(seq), P(seq), P())
    )
    return jax.shard_map(
        local,
        mesh=split,
        in_specs=placed,
        out_specs=(tokens, P(), tokens)
        + (weight,) * 8
        + (P(seq, None), P(None, "c"), P("c"), P(seq), P(seq), P()),
        check_vma=False,
    )
```
